512 devices in a mesh: row: 32 (over x_hi, z), col: 16 (over x_lo, y, core).
Axes of the slice: x: 4 (x_hi: 2, x_lo: 2; x = x_hi * 2 + x_lo), y: 4, z: 16, core: 2. Of those that a mesh axis runs over, the one named last changes fastest.
Arguments:
- trailing: float32 [64, 16, 512, 512], P('row', 'col'), may hold values from -6 to 6
- panel_block: float32 [64, 512, 1024], P('row', 'col'), may hold values from -2.5 to 2.5
- diag_block: float32 [1024, 1024], P('row'), as said below
- tile_map: int32 [64], replicated, may hold values from 0 to 63, each once
Outputs:
- updated_trailing: float32 [64, 16, 512, 512], P('row', 'col')
- panel_factor: float32 [64, 512, 1024], P('row', 'col')
- diag_factor: float32 [1024, 1024], P('row')
The draws below stay inside these ranges and needn't reach their ends.
Inputs may be any that keep to these rules, and one draw needn't show every extreme that they name: `tile_map`: each of the 64 trailing tile rows stands in exactly one slot. `diag_block`: symmetric and positive definite.
All inputs are finite; a program needn't handle non-finite values.
Results may differ from the reference program's by a relative error of at most 0.0003.
Values sent between devices are 32-bit elements; how exact they have to be, the bound alone decides.
A program may use at most 128 MiB of HBM per device.

```python
import jax
import jax.numpy as jnp
from jax import lax

TILE = 512
PW = 1024
NT = 64
N_COL = 16


def draw_diag_block(key, part):
    key_values, key_diag = jax.random.split(jax.random.fold_in(key, 7), 2)
    uniform_draw = jax.random.uniform(key_values, (PW, PW), jnp.float32, -1.0, 1.0)
    spread = 0.25 * 1.5 ** 0.5 / PW ** 0.5
    symmetric = (uniform_draw + uniform_draw.T) * spread
    identity = jnp.eye(PW, dtype=jnp.float32)
    diag_lift = jax.random.uniform(key_diag, (PW,), jnp.float32, 1.0, 2.0)
    matrix = symmetric * (1.0 - identity) + identity * diag_lift[None, :]
    return matrix


def levels(rng, shape, pieces, smallest, high):
    level = 1.0
    for position, blocks in pieces:
        steps = jax.random.uniform(jax.random.fold_in(jax.random.fold_in(rng, 6), position), (blocks,), jnp.float32, smallest / len(pieces), high / len(pieces))
        level = level * jnp.repeat(jnp.exp(steps), shape[position] // blocks).reshape((-1,) + (1,) * (len(shape) - 1 - position))
    return level


def bell_draw(rng, dims, deviation, most, pieces=(), held_as=jnp.bfloat16):
    drawn = jax.random.normal(rng, dims, jnp.float32) * deviation
    if len(pieces) > 0:
        drawn = levels(rng, dims, pieces, -0.22, 0.18) * drawn
    return jnp.clip(drawn, min=-most, max=most).astype(held_as)


def setup_inputs(seed: int = 0) -> dict:
    streams_of = jax.random.split(jax.random.key(seed), 5)
    return {
        "trailing": bell_draw(streams_of[0], (NT, N_COL, TILE, TILE), 1.0, 6.0, ((0, 32), (1, 16)), jnp.float32),
        "panel_block": bell_draw(streams_of[1], (NT, TILE, PW), 0.18, 2.5, ((0, 32), (1, 16)), jnp.float32),
        "diag_block": draw_diag_block(jax.random.fold_in(streams_of[4], 71), 0),
        "tile_map": jax.random.permutation(streams_of[3], NT).astype(jnp.int32),
    }


def solve_rows(factor, row_block):
    flattened = row_block.reshape(-1, row_block.shape[-1])
    solved = lax.linalg.triangular_solve(factor, flattened, left_side=False, lower=True, transpose_a=True)
    return solved.reshape(row_block.shape)

def reference(trailing, panel_block, diag_block, tile_map):
    diag_factor = jnp.linalg.cholesky(diag_block)
    panel_factor = solve_rows(diag_factor, panel_block)
    slot_index = jnp.arange(tile_map.shape[0], dtype=jnp.int32)
    column_ids = jnp.arange(N_COL, dtype=jnp.int32)
    owner_slot = jnp.sum(jnp.where(tile_map[None, :] == column_ids[:, None], slot_index[None, :], 0), axis=1).astype(jnp.int32)
    column_panel = panel_factor[owner_slot]

    def update(slot_data):
        tile_rows, slot_panel, tile_id = slot_data
        products = jnp.einsum('ak,cbk->cab', slot_panel, column_panel, precision=lax.Precision.HIGHEST)
        tile_live = tile_id >= column_ids
        return jnp.where(tile_live[:, None, None], tile_rows - products, jnp.zeros_like(tile_rows))
    updated_trailing = lax.map(update, (trailing, panel_factor, tile_map))
    return (updated_trailing, panel_factor, diag_factor)
```

```python
import jax
import jax.numpy as jnp
from jax import lax
from jax.experimental import pallas as pl
from jax.experimental.pallas import tpu as pltpu
from jax.sharding import PartitionSpec as P

F32 = jnp.float32
BF16 = jnp.bfloat16
MESH = pl.DeviceIdType.MESH
NB = 8
BS = 128


def dot_nt(a, b):
    return lax.dot_general(
        a, b, (((1,), (1,)), ((), ())),
        precision=lax.Precision.HIGHEST, preferred_element_type=F32,
    )


def dot_nn(a, b):
    return lax.dot_general(
        a, b, (((1,), (0,)), ((), ())),
        precision=lax.Precision.HIGHEST, preferred_element_type=F32,
    )


def split(x):
    hi = x.astype(BF16)
    return hi, (x - hi.astype(F32)).astype(BF16)


def dot3(ah, al, bh, bl):
    def one(a, b):
        return lax.dot_general(
            a, b, (((1,), (1,)), ((), ())), preferred_element_type=F32
        )
    return one(ah, bh) + (one(ah, bl) + one(al, bh))


def factor_block(d_ref, w_ref):
    iota = lax.broadcasted_iota(jnp.int32, (8, BS), 0)
    lane = lax.broadcasted_iota(jnp.int32, (8, BS), 1)
    groups = BS // 8

    def row(x, j):
        return jnp.broadcast_to(x[j:j + 1, :], (8, BS))

    def column(x, j):
        return jnp.broadcast_to(x[:, j:j + 1], (8, BS))

    for q in range(groups):
        w_ref[8 * q:8 * q + 8, :] = jnp.where(lane == iota + 8 * q, 1.0, 0.0).astype(F32)
    for p in range(groups):
        base = 8 * p
        rows = slice(base, base + 8)
        d = d_ref[rows, :]
        w = w_ref[rows, :]
        cols = [column(d, base + k) for k in range(8)]
        inverse, pivots, heads = [], [], []
        for j in range(8):
            pivot = row(cols[j], j)
            inv = 1.0 / pivot
            pivots.append(pivot)
            inverse.append(inv)
            below = jnp.where(iota > j, cols[j], 0.0)
            head = [None] * 8
            for k in range(j + 1, 8):
                head[k] = row(cols[k], j)
                cols[k] = cols[k] - (below * head[k]) * inv
            heads.append(head)
            m = below * inv
            d = d - m * row(d, j)
            w = w - m * row(w, j)
        d_rows = [row(d, j) for j in range(8)]
        w_rows = [row(w, j) for j in range(8)]
        diag = pivots[7]
        for j in range(7):
            diag = jnp.where(iota == j, pivots[j], diag)
        scale = lax.rsqrt(diag)
        d_ref[rows, :] = jnp.where(lane >= iota + base, d * scale, 0.0)
        w_ref[rows, :] = w * scale
        for q in range(p + 1, groups):
            part = slice(8 * q, 8 * q + 8)
            dq = d_ref[part, :]
            wq = w_ref[part, :]
            cq = [column(dq, base + k) for k in range(8)]
            for j in range(8):
                mq = cq[j] * inverse[j]
                for k in range(j + 1, 8):
                    cq[k] = cq[k] - mq * heads[j][k]
                dq = dq - mq * d_rows[j]
                wq = wq - mq * w_rows[j]
            d_ref[part, :] = dq
            w_ref[part, :] = wq


def kernel(
    tm_ref, a_in, b_in, t_hbm,
    out_hbm, pf_out, df_out,
    a_ref, l_ref, w_ref, cbuf, rp, cp, rsp, rsm, xh_own, xh_got, items,
    xhi, xlo, lhi, llo, tbuf,
    t_sem, o_sem, loc, s1, r1, s2, r2, s3, r3, sb, rb, srs, rrs, sx, rx, sag, rag, sa, ra,
):
    me_row = lax.axis_index("row")
    me_col = lax.axis_index("col")
    h, z = me_row // 16, me_row % 16
    l, y, k = me_col // 8, (me_col // 2) % 4, me_col % 2
    zq, zr = z // 4, z % 4
    turn = 2 * k + l
    plane = h * 8 + l * 4 + y
    chip = l * 4 + y
    sib = me_col + 1 - 2 * k
    t0 = tm_ref[2 * me_row]
    t1 = tm_ref[2 * me_row + 1]

    def remote(src, dst, ssem, rsem, row, col):
        return pltpu.make_async_remote_copy(
            src_ref=src, dst_ref=dst, send_sem=ssem, recv_sem=rsem,
            device_id={"row": row, "col": col}, device_id_type=MESH,
        )

    def greet(row, col):
        pl.semaphore_signal(
            pltpu.get_barrier_semaphore(), inc=1,
            device_id={"row": row, "col": col}, device_id_type=MESH,
        )

    tcopies = [pltpu.make_async_copy(t_hbm.at[s], tbuf.at[s], t_sem.at[s]) for s in range(2)]
    for cpy in tcopies:
        cpy.start()

    @pl.loop(1, 16)
    def _(d):
        greet(h * 16 + (z + d) % 16, me_col)

    @pl.loop(1, 32)
    def _(d):
        q = (h * 16 + me_col + d) % 32
        greet((q // 16) * 16 + z, q % 16)

    pl.semaphore_wait(pltpu.get_barrier_semaphore(), 46)

    def a1(d):
        return remote(a_in.at[y], a_ref.at[h, zq, zr, y], s1.at[d], r1.at[zq],
                      h * 16 + (z + d) % 16, me_col)

    a_local = pltpu.make_async_copy(a_in.at[y], a_ref.at[h, zq, zr, y], loc.at[0])

    def a1_start():
        @pl.when(zr == turn)
        def _():
            a_local.start()

            @pl.loop(1, 16)
            def _(d):
                a1(d).start()

    def a1_wait():
        @pl.loop(0, 4)
        def _(q):
            @pl.when(q * 4 + turn != z)
            def _():
                pltpu.make_async_copy(
                    a_ref.at[h, q, turn, y], a_ref.at[h, q, turn, y], r1.at[q]).wait()

        @pl.when(zr == turn)
        def _():
            a_local.wait()

    def lanes(J):
        return slice(BS * J, BS * J + BS)

    def first(J, hh):
        return min(max(J - 4 * hh, 0), 4)

    def a2(J, hh, d):
        q = (plane + d) % 16
        sl = a_ref.at[hh, first(J, hh):4, turn, y, :, lanes(J)]
        return remote(sl, sl, s2.at[d], r2.at[J, plane],
                      (q // 8) * 16 + z, (q % 8) * 2 + k)

    def a2_start(J):
        for hh in range(2):
            if first(J, hh) < 4:
                @pl.when(h == hh)
                def _(hh=hh):
                    @pl.loop(1, 16)
                    def _(d):
                        a2(J, hh, d).start()

    def a2_sent(J):
        for hh in range(2):
            if first(J, hh) < 4:
                @pl.when(h == hh)
                def _(hh=hh):
                    @pl.loop(1, 16)
                    def _(d):
                        a2(J, hh, d).wait_send()

    def a2_wait(J):
        for hh in range(2):
            if first(J, hh) < 4:
                @pl.loop(0, 8)
                def _(c, hh=hh):
                    @pl.when(hh * 8 + c != plane)
                    def _():
                        sl = a_ref.at[hh, first(J, hh):4, 2 * k + c // 4, c % 4, :, lanes(J)]
                        pltpu.make_async_copy(sl, sl, r2.at[J, hh * 8 + c]).wait()

    def a3(J, hh, kk):
        sl = a_ref.at[hh, first(J, hh):4, pl.ds(2 * kk, 2), :, :, lanes(J)]
        return remote(sl, sl, s3.at[J, hh], r3.at[J, hh], me_row, sib)

    def a3_start(J):
        for hh in range(2):
            if first(J, hh) < 4:
                a3(J, hh, k).start()

    def a3_wait(J):
        for hh in range(2):
            if first(J, hh) < 4:
                a3(J, hh, 1 - k).wait_recv()

    def a3_sent(J):
        for hh in range(2):
            if first(J, hh) < 4:
                a3(J, hh, k).wait_send()

    def b1(d):
        q = (chip + d) % 8
        return remote(b_in, rp.at[:, l, y, k], sb.at[d], rb.at[chip], me_row, q * 2 + k)

    b_local = pltpu.make_async_copy(b_in, rp.at[:, l, y, k], loc.at[1])

    def b1_start():
        b_local.start()

        @pl.loop(1, 8)
        def _(d):
            b1(d).start()

    def b1_wait():
        b_local.wait()

        @pl.loop(0, 8)
        def _(c):
            @pl.when(c != chip)
            def _():
                sl = rp.at[:, c // 4, c % 4, k]
                pltpu.make_async_copy(sl, sl, rb.at[c]).wait()

        @pl.loop(1, 8)
        def _(d):
            b1(d).wait_send()

    def b2(kk):
        return remote(rp.at[:, :, :, kk], rp.at[:, :, :, kk], sb.at[0], rb.at[8], me_row, sib)

    right = h * 16 + (z + 1) % 16
    left = h * 16 + (z + 15) % 16
    NS = 2

    def part(n):
        return pl.ds(n * (32 // NS), 32 // NS)

    def rs(way, t, n):
        buf = rsm if way else rsp
        return remote(buf.at[t, part(n)], buf.at[t + 1, part(n)],
                      srs.at[way, t, n], rrs.at[way, t, n], left if way else right, me_col)

    def rs_step(t):
        for n in range(NS):
            for way in range(2):
                if t < 8 - way:
                    buf = rsm if way else rsp
                    item = (z + 9 + t) % 16 if way else (z + 8 - t + 16) % 16
                    if t > 0:
                        rs(way, t - 1, n).wait_recv()
                    own = b_in[1, part(n), :]
                    own0 = b_in[0, part(n), :]
                    if t > 0:
                        other = jnp.where(t0 == item, own0, buf[t, part(n), :])
                    else:
                        other = own0
                    buf[t, part(n), :] = jnp.where(t1 == item, own, other)
                    rs(way, t, n).start()

    def owner_of(item):
        def look(i, best):
            return jnp.where(tm_ref[i] == item, i, best)
        return lax.fori_loop(0, 64, look, jnp.int32(0))

    slot = owner_of(z)
    oh, oz = slot // 32, (slot // 2) % 16
    gap = (oz - z + 16) % 16

    def x1(n):
        return remote(xh_own.at[part(n)], xh_got.at[part(n)], sx.at[n], rx.at[n],
                      (1 - h) * 16 + z, me_col)

    def collect(n):
        rs(0, 7, n).wait_recv()
        rs(1, 6, n).wait_recv()
        own = jnp.where(slot % 2 == 1, b_in[1, part(n), :], b_in[0, part(n), :])
        chain = jnp.where(gap >= 8, rsp[8, part(n), :], rsm[7, part(n), :])
        xh_own[part(n), :] = jnp.where(gap == 0, own, chain)
        x1(n).start()

    def ag(way, t, n):
        item = (z + t) % 16 if way else (z - t + 16) % 16
        sl = items.at[item, part(n)]
        return remote(sl, sl, sag.at[way, t, n], rag.at[way, t, n],
                      left if way else right, me_col)

    def ag_got(way, t, n):
        item = (z + 1 + t) % 16 if way else (z - 1 - t + 32) % 16
        sl = items.at[item, part(n)]
        return pltpu.make_async_copy(sl, sl, rag.at[way, t, n])

    def a2a(item):
        return remote(items.at[item], cp.at[me_col], sa.at[item], ra.at[me_col], me_row, item)

    def a2a_local():
        return pltpu.make_async_copy(items.at[me_col], cp.at[me_col], loc.at[2])

    def a2a_start(item):
        @pl.when(item == me_col)
        def _():
            a2a_local().start()

        @pl.when(item != me_col)
        def _():
            a2a(item).start()

    def chosen(n):
        x1(n).wait_recv()
        items[z, part(n), :] = jnp.where(oh == h, xh_own[part(n), :], xh_got[part(n), :])
        for way in range(2):
            ag(way, 0, n).start()

    def ag_step(t):
        for n in range(NS):
            for way in range(2):
                if t - 1 < 8 - way:
                    ag_got(way, t - 1, n).wait()
                    if t < 8 - way:
                        ag(way, t, n).start()
        for way in range(2):
            if t - 1 < 8 - way:
                a2a_start((z + t) % 16 if way else (z - t + 16) % 16)

    def a2a_wait():
        @pl.loop(0, 16)
        def _(c):
            @pl.when(c == me_col)
            def _():
                a2a_local().wait()

            @pl.when(c != me_col)
            def _():
                pltpu.make_async_copy(cp.at[c], cp.at[c], ra.at[c]).wait()
                a2a(c).wait_send()

    def sends_done():
        @pl.when(zr == turn)
        def _():
            @pl.loop(1, 16)
            def _(d):
                a1(d).wait_send()
        a2_sent(7)
        for J in range(8):
            a3_sent(J)
        for n in range(NS):
            for way in range(2):
                for t in range(8 - way):
                    rs(way, t, n).wait_send()
                    ag(way, t, n).wait_send()
            x1(n).wait_send()

    def head():
        a1_start()
        rs_step(0)
        b1_start()
        a1_wait()
        a2_start(0)
        a2_wait(0)
        a3_start(0)
        a2_sent(0)
        a2_start(1)

    def tick(J, half):
        step = 2 * J + half + 1
        if half == 0:
            if J < 7:
                a2_wait(J + 1)
                a3_start(J + 1)
                if J < 6:
                    a2_sent(J + 1)
                    a2_start(J + 2)
        if J == 3 and half == 1:
            b1_wait()
            b2(k).start()
        if step <= 7:
            rs_step(step)
        elif step == 8:
            for n in range(NS):
                collect(n)
        elif step == 9:
            for n in range(NS):
                chosen(n)
            a2a_start(z)
        else:
            ag_step(step - 9)

    head()

    l_ref[...] = jnp.zeros_like(l_ref)

    def block(I, J):
        return a_ref[I // 4, I % 4, :, :, :, lanes(J)].reshape(BS, BS)

    @pl.loop(0, NB)
    def _(Jd):
        for J in range(NB):
            @pl.when(Jd == J)
            def _(J=J):
                a3_wait(J)
                own = slice(BS * J, BS * J + BS)
                c = jnp.concatenate([block(I, J) for I in range(J, NB)], axis=0)
                if J > 0:
                    c = c - dot_nt(l_ref[BS * J:, :BS * J], l_ref[own, :BS * J])
                cbuf[:BS * (NB - J), :] = c
                tick(J, 0)
        factor_block(cbuf.at[0:BS], w_ref.at[Jd])
        for J in range(NB):
            @pl.when(Jd == J)
            def _(J=J):
                tick(J, 1)
                own = slice(BS * J, BS * J + BS)
                l_ref[own, own] = cbuf[:BS, :].T
                if J < NB - 1:
                    l_ref[BS * (J + 1):, own] = dot_nt(cbuf[BS:BS * (NB - J), :], w_ref[J])

    ag_step(8)
    a2a_wait()
    b2(k).wait_send()
    b2(1 - k).wait_recv()

    df_out[...] = l_ref[pl.ds(pl.multiple_of(me_row * 32, 32), 32), :]
    hi, lo = split(l_ref[...])
    lhi[...] = hi
    llo[...] = lo
    for m in range(4):
        cs = slice(256 * m, 256 * m + 256)
        w0, w1 = w_ref[2 * m], w_ref[2 * m + 1]
        l10 = l_ref[256 * m + BS:256 * m + 256, 256 * m:256 * m + BS]
        w10 = -dot_nn(w1, dot_nn(l10, w0))
        wide = jnp.concatenate([
            jnp.concatenate([w0, jnp.zeros_like(w0)], axis=1),
            jnp.concatenate([w10, w1], axis=1)], axis=0)
        wh, wl = split(wide)
        for g in range(3):
            rows = slice(512 * g, 512 * g + 512)
            if g < 2:
                v = rp[g, :, :, :, :, cs].reshape(512, 256)
            else:
                v = cp[:, :, cs].reshape(512, 256)
            if m > 0:
                v = v - dot3(xhi[rows, :256 * m], xlo[rows, :256 * m],
                             lhi[cs, :256 * m], llo[cs, :256 * m])
            vh, vl = split(v)
            x = dot3(vh, vl, wh, wl)
            if g < 2:
                rp[g, :, :, :, :, cs] = x.reshape(2, 4, 2, 32, 256)
            hi, lo = split(x)
            xhi[rows, cs] = hi
            xlo[rows, cs] = lo
    for s in range(2):
        pf_out[s] = rp[s, l, y, k]

    for s in range(2):
        tcopies[s].wait()
        live = (t1 if s else t0) >= me_col
        rows = slice(512 * s, 512 * s + 512)
        prod = dot3(xhi[rows, :], xlo[rows, :], xhi[1024:, :], xlo[1024:, :])
        tbuf[s] = jnp.where(live, tbuf[s] - prod, 0.0)
        pltpu.make_async_copy(tbuf.at[s], out_hbm.at[s], o_sem.at[s]).start()
    sends_done()
    for s in range(2):
        pltpu.make_async_copy(tbuf.at[s], out_hbm.at[s], o_sem.at[s]).wait()


def per_device(trailing, panel_block, diag_block, tile_map):
    sem = pltpu.SemaphoreType.DMA
    vm = pl.BlockSpec(memory_space=pltpu.VMEM)
    updated, piece, diag = pl.pallas_call(
        kernel,
        out_shape=(
            jax.ShapeDtypeStruct((2, 512, 512), F32),
            jax.ShapeDtypeStruct((2, 32, 1024), F32),
            jax.ShapeDtypeStruct((32, 1024), F32),
        ),
        in_specs=[pl.BlockSpec(memory_space=pltpu.SMEM), vm, vm, pl.BlockSpec(memory_space=pl.ANY)],
        out_specs=(pl.BlockSpec(memory_space=pl.ANY), vm, vm),
        scratch_shapes=[
            pltpu.VMEM((2, 4, 4, 4, 8, 1024), F32),
            pltpu.VMEM((1024, 1024), F32),
            pltpu.VMEM((NB, BS, BS), F32),
            pltpu.VMEM((1024, BS), F32),
            pltpu.VMEM((2, 2, 4, 2, 32, 1024), F32),
            pltpu.VMEM((16, 32, 1024), F32),
            pltpu.VMEM((9, 32, 1024), F32),
            pltpu.VMEM((8, 32, 1024), F32),
            pltpu.VMEM((32, 1024), F32),
            pltpu.VMEM((32, 1024), F32),
            pltpu.VMEM((16, 32, 1024), F32),
            pltpu.VMEM((1536, 1024), BF16),
            pltpu.VMEM((1536, 1024), BF16),
            pltpu.VMEM((1024, 1024), BF16),
            pltpu.VMEM((1024, 1024), BF16),
            pltpu.VMEM((2, 512, 512), F32),
            sem((2,)), sem((2,)), sem((3,)),
            sem((16,)), sem((4,)), sem((16,)), sem((8, 16)), sem((8, 2)), sem((8, 2)),
            sem((8,)), sem((9,)), sem((2, 8, 2)), sem((2, 8, 2)), sem((2,)), sem((2,)),
            sem((2, 8, 2)), sem((2, 8, 2)), sem((16,)), sem((16,)),
        ],
        compiler_params=pltpu.CompilerParams(
            collective_id=0, has_side_effects=True, vmem_limit_bytes=60 << 20
        ),
    )(tile_map, diag_block.reshape(4, 8, 1024), panel_block, trailing[:, 0])
    return (updated[:, None], piece, diag)


def solution(mesh):
    in_specs = (P("row", "col", None, None), P("row", "col", None), P("row", None), P())
    out_specs = (P("row", "col", None, None), P("row", "col", None), P("row", None))
    return jax.shard_map(
        per_device, mesh=mesh, in_specs=in_specs, out_specs=out_specs, check_vma=False
    )
```

```python
import jax
import jax.numpy as jnp
from jax import lax
from jax.experimental import pallas as pl
from jax.experimental.pallas import tpu as pltpu
from jax.sharding import PartitionSpec as P

F32 = jnp.float32
BF16 = jnp.bfloat16
MESH = pl.DeviceIdType.MESH
NB = 8
BS = 128


def dot_nt(a, b):
    return lax.dot_general(
        a, b, (((1,), (1,)), ((), ())),
        precision=lax.Precision.HIGHEST, preferred_element_type=F32,
    )


def dot_nn(a, b):
    return lax.dot_general(
        a, b, (((1,), (0,)), ((), ())),
        precision=lax.Precision.HIGHEST, preferred_element_type=F32,
    )


def split(x):
    hi = x.astype(BF16)
    return hi, (x - hi.astype(F32)).astype(BF16)


def dot3(ah, al, bh, bl):
    def one(a, b):
        return lax.dot_general(
            a, b, (((1,), (1,)), ((), ())), preferred_element_type=F32
        )
    return one(ah, bh) + (one(ah, bl) + one(al, bh))


def factor_block(d_ref, w_ref, begin, end):
    iota = lax.broadcasted_iota(jnp.int32, (8, BS), 0)
    lane = lax.broadcasted_iota(jnp.int32, (8, BS), 1)
    groups = BS // 8

    def row(x, j):
        return jnp.broadcast_to(x[j:j + 1, :], (8, BS))

    def column(x, j):
        return jnp.broadcast_to(x[:, j:j + 1], (8, BS))

    if begin == 0:
        for q in range(groups):
            w_ref[8 * q:8 * q + 8, :] = jnp.where(lane == iota + 8 * q, 1.0, 0.0).astype(F32)
    for p in range(begin, end):
        base = 8 * p
        rows = slice(base, base + 8)
        d = d_ref[rows, :]
        w = w_ref[rows, :]
        cols = [column(d, base + k) for k in range(8)]
        inverse, pivots, heads = [], [], []
        for j in range(8):
            pivot = row(cols[j], j)
            inv = 1.0 / pivot
            pivots.append(pivot)
            inverse.append(inv)
            below = jnp.where(iota > j, cols[j], 0.0)
            head = [None] * 8
            for k in range(j + 1, 8):
                head[k] = row(cols[k], j)
                cols[k] = cols[k] - (below * head[k]) * inv
            heads.append(head)
            m = below * inv
            d = d - m * row(d, j)
            w = w - m * row(w, j)
        d_rows = [row(d, j) for j in range(8)]
        w_rows = [row(w, j) for j in range(8)]
        diag = pivots[7]
        for j in range(7):
            diag = jnp.where(iota == j, pivots[j], diag)
        scale = lax.rsqrt(diag)
        d_ref[rows, :] = jnp.where(lane >= iota + base, d * scale, 0.0)
        w_ref[rows, :] = w * scale
        for q in range(p + 1, groups):
            part = slice(8 * q, 8 * q + 8)
            dq = d_ref[part, :]
            wq = w_ref[part, :]
            cq = [column(dq, base + k) for k in range(8)]
            for j in range(8):
                mq = cq[j] * inverse[j]
                for k in range(j + 1, 8):
                    cq[k] = cq[k] - mq * heads[j][k]
                dq = dq - mq * d_rows[j]
                wq = wq - mq * w_rows[j]
            d_ref[part, :] = dq
            w_ref[part, :] = wq


def kernel(
    tm_ref, a_in, b_in, t_hbm,
    out_hbm, pf_out, df_out,
    a_ref, l_ref, w_ref, cbuf, rp, cp, bx, rsp, rsm, items,
    xs, xo, xhi, xlo, lhi, llo, tbuf,
    t_sem, o_sem, loc, s1, r1, s2, r2, s3, r3, sb, rb, srs, rrs, sx, rx, sag, rag, sa, ra,
    sxx, rxx,
):
    me_row = lax.axis_index("row")
    me_col = lax.axis_index("col")
    h, z = me_row // 16, me_row % 16
    l, y, k = me_col // 8, (me_col // 2) % 4, me_col % 2
    zq, zr = z // 4, z % 4
    turn = 2 * k + l
    plane = h * 8 + l * 4 + y
    chip = l * 4 + y
    sib = me_col + 1 - 2 * k

    def remote(src, dst, ssem, rsem, row, col):
        return pltpu.make_async_remote_copy(
            src_ref=src, dst_ref=dst, send_sem=ssem, recv_sem=rsem,
            device_id={"row": row, "col": col}, device_id_type=MESH,
        )

    def greet(row, col):
        pl.semaphore_signal(
            pltpu.get_barrier_semaphore(), inc=1,
            device_id={"row": row, "col": col}, device_id_type=MESH,
        )

    @pl.loop(0, 15)
    def _(i):
        d = 8 + (i + 1) // 2 * (1 - 2 * (i % 2))
        greet(h * 16 + (z + d) % 16, me_col)

    @pl.loop(1, 32)
    def _(d):
        q = (h * 16 + me_col + d) % 32
        greet((q // 16) * 16 + z, q % 16)

    def t_copy(g):
        slot = k if g == 0 else 1 - k
        return pltpu.make_async_copy(t_hbm.at[slot], tbuf.at[g], t_sem.at[g])

    def o_copy(g):
        slot = k if g == 0 else 1 - k
        return pltpu.make_async_copy(tbuf.at[g], out_hbm.at[slot], o_sem.at[g])

    for s in range(2):
        t_copy(s).start()

    pl.semaphore_wait(pltpu.get_barrier_semaphore(), 46)

    def lanes(J):
        return slice(BS * J, BS * J + BS)

    pieces = (slice(0, BS), slice(BS, NB * BS))

    def a1(n, d):
        return remote(a_in.at[y, :, pieces[n]], a_ref.at[h, zq, zr, y, :, pieces[n]],
                      s1.at[n, d], r1.at[n, zq], h * 16 + (z + d) % 16, me_col)

    def a_local(n):
        return pltpu.make_async_copy(
            a_in.at[y, :, pieces[n]], a_ref.at[h, zq, zr, y, :, pieces[n]], loc.at[n])

    def a1_start(n):
        @pl.when(zr == turn)
        def _():
            a_local(n).start()

            @pl.loop(0, 15)
            def _(i):
                a1(n, 8 + (i + 1) // 2 * (1 - 2 * (i % 2))).start()

    def a1_wait(n):
        @pl.loop(0, 4)
        def _(q):
            @pl.when(q * 4 + turn != z)
            def _():
                sl = a_ref.at[h, q, turn, y, :, pieces[n]]
                pltpu.make_async_copy(sl, sl, r1.at[n, q]).wait()

        @pl.when(zr == turn)
        def _():
            a_local(n).wait()

    def first(J, hh):
        return min(max(J - 4 * hh, 0), 4)

    def a2(J, hh, d):
        q = (plane + d) % 16
        sl = a_ref.at[hh, first(J, hh):4, turn, y, :, lanes(J)]
        return remote(sl, sl, s2.at[J, d], r2.at[J, plane],
                      (q // 8) * 16 + z, (q % 8) * 2 + k)

    def a2_each(J, act):
        for hh in range(2):
            if first(J, hh) < 4:
                @pl.when(h == hh)
                def _(hh=hh):
                    @pl.loop(1, 16)
                    def _(d):
                        act(a2(J, hh, d))

    def a2_start(J):
        a2_each(J, lambda c: c.start())

    def a2_sent(J):
        a2_each(J, lambda c: c.wait_send())

    def a2_wait(J):
        for hh in range(2):
            if first(J, hh) < 4:
                @pl.loop(0, 8)
                def _(c, hh=hh):
                    @pl.when(hh * 8 + c != plane)
                    def _():
                        sl = a_ref.at[hh, first(J, hh):4, 2 * k + c // 4, c % 4, :, lanes(J)]
                        pltpu.make_async_copy(sl, sl, r2.at[J, hh * 8 + c]).wait()

    def a3(J, hh, kk):
        sl = a_ref.at[hh, first(J, hh):4, pl.ds(2 * kk, 2), :, :, lanes(J)]
        return remote(sl, sl, s3.at[J, hh], r3.at[J, hh], me_row, sib)

    def halves(J):
        return [hh for hh in range(2) if first(J, hh) < 4]

    def a3_start(J):
        for hh in halves(J):
            a3(J, hh, k).start()

    def a3_wait(J):
        for hh in halves(J):
            a3(J, hh, 1 - k).wait_recv()

    def a3_sent(J):
        for hh in halves(J):
            a3(J, hh, k).wait_send()

    def b1(d, s):
        q = (chip + d) % 8
        return remote(b_in.at[s], rp.at[l, y, k], sb.at[d, s], rb.at[me_col],
                      me_row, q * 2 + s)

    def b_local():
        return pltpu.make_async_copy(b_in.at[k], rp.at[l, y, k], loc.at[2])

    def b1_each(act):
        for s in range(2):
            @pl.when(s != k)
            def _(s=s):
                act(b1(0, s))

            @pl.loop(1, 8)
            def _(d, s=s):
                act(b1(d, s))

    def b1_start():
        b_local().start()
        b1_each(lambda c: c.start())

    def b1_wait():
        b_local().wait()

        @pl.loop(0, 16)
        def _(c):
            @pl.when(c != me_col)
            def _():
                sl = rp.at[c // 8, (c // 2) % 4, c % 2]
                pltpu.make_async_copy(sl, sl, rb.at[c]).wait()

    right = h * 16 + (z + 1) % 16
    left = h * 16 + (z + 15) % 16
    NS = 2
    HR = 16
    ids = [tm_ref[2 * z], tm_ref[2 * z + 1], tm_ref[2 * z + 32], tm_ref[2 * z + 33]]

    def part(n):
        return pl.ds(n * (HR // NS), HR // NS)

    def swap():
        return remote(b_in.at[:, pl.ds((1 - h) * HR, HR)], bx.at[h], sx.at[0], rx.at[0],
                      (1 - h) * 16 + z, me_col)

    def swap_local():
        return pltpu.make_async_copy(b_in.at[:, pl.ds(h * HR, HR)], bx.at[h], loc.at[3])

    def swap_start():
        swap().start()
        swap_local().start()

    def swap_wait():
        swap_local().wait()
        sl = bx.at[1 - h]
        pltpu.make_async_copy(sl, sl, rx.at[0]).wait()

    def pick(item, n, value):
        for i in range(4):
            value = jnp.where(ids[i] == item, bx[i // 2, i % 2, part(n), :], value)
        return value

    def rs(way, t, n):
        buf = rsm if way else rsp
        return remote(buf.at[t, part(n)], buf.at[t + 1, part(n)],
                      srs.at[way, t, n], rrs.at[way, t, n], left if way else right, me_col)

    def rs_step(t):
        for n in range(NS):
            for way in range(2):
                if t < 8 - way:
                    buf = rsm if way else rsp
                    item = (z + 9 + t) % 16 if way else (z + 8 - t + 16) % 16
                    if t > 0:
                        rs(way, t - 1, n).wait_recv()
                        came = buf[t, part(n), :]
                    else:
                        came = bx[0, 0, part(n), :]
                    buf[t, part(n), :] = pick(item, n, came)
                    rs(way, t, n).start()

    def owner_of(item):
        def look(i, best):
            return jnp.where(tm_ref[i] == item, i, best)
        return lax.fori_loop(0, 64, look, jnp.int32(0))

    def ag(way, t, n):
        item = (z + t) % 16 if way else (z - t + 16) % 16
        sl = items.at[item, part(n)]
        return remote(sl, sl, sag.at[way, t, n], rag.at[way, t, n],
                      left if way else right, me_col)

    def ag_got(way, t, n):
        item = (z + 1 + t) % 16 if way else (z - 1 - t + 32) % 16
        sl = items.at[item, part(n)]
        return pltpu.make_async_copy(sl, sl, rag.at[way, t, n])

    def hand(item, hh):
        return remote(items.at[item], cp.at[me_col, h], sa.at[item, hh], ra.at[me_col, h],
                      hh * 16 + z, item)

    def hand_local():
        return pltpu.make_async_copy(items.at[me_col], cp.at[me_col, h], loc.at[4])

    def hand_each(item, act, act_local):
        if act_local is not None:
            @pl.when(item == me_col)
            def _():
                act_local(hand_local())

        @pl.when(item != me_col)
        def _():
            act(hand(item, h))
        act(hand(item, 1 - h))

    def hand_start(item):
        hand_each(item, lambda c: c.start(), lambda c: c.start())

    def collect():
        slot = owner_of(z)
        gap = ((slot // 2) % 16 - z + 16) % 16
        for n in range(NS):
            rs(0, 7, n).wait_recv()
            rs(1, 6, n).wait_recv()
            chain = jnp.where(gap >= 8, rsp[8, part(n), :], rsm[7, part(n), :])
            items[z, part(n), :] = pick(z, n, chain)
            for way in range(2):
                ag(way, 0, n).start()
        hand_start(z)

    def ag_step(t):
        for n in range(NS):
            for way in range(2):
                if t - 1 < 8 - way:
                    ag_got(way, t - 1, n).wait()
                    if t < 8 - way:
                        ag(way, t, n).start()
        for way in range(2):
            if t - 1 < 8 - way:
                hand_start((z + t) % 16 if way else (z - t + 16) % 16)

    def hand_wait():
        hand_local().wait()
        for hh in range(2):
            @pl.loop(0, 16)
            def _(c, hh=hh):
                @pl.when((c != me_col) | (h != hh))
                def _():
                    pltpu.make_async_copy(cp.at[c, hh], cp.at[c, hh], ra.at[c, hh]).wait()

    def xx(m):
        return remote(xs.at[m], xo.at[m], sxx.at[m], rxx.at[m], me_row, sib)

    def sends_done():
        @pl.when(zr == turn)
        def _():
            for n in range(2):
                @pl.loop(1, 16)
                def _(d, n=n):
                    a1(n, d).wait_send()
        for J in range(NB):
            a2_sent(J)
            a3_sent(J)
        b1_each(lambda c: c.wait_send())
        swap().wait_send()
        for n in range(NS):
            for way in range(2):
                for t in range(8 - way):
                    rs(way, t, n).wait_send()
                    ag(way, t, n).wait_send()

        @pl.loop(0, 16)
        def _(c):
            hand_each(c, lambda q: q.wait_send(), None)
        for m in range(4):
            xx(m).wait_send()

    def head():
        a1_start(0)
        swap_start()
        a1_start(1)
        swap_wait()
        rs_step(0)
        a1_wait(0)
        a2_start(0)
        rs_step(1)
        a1_wait(1)
        for J in range(1, 4):
            a2_start(J)
        rs_step(2)
        a2_wait(0)
        a3_start(0)
        for J in range(4, NB):
            a2_start(J)
        b1_start()

    def tick(J, half):
        if half == 1 and J < NB - 1:
            a2_wait(J + 1)
            a3_start(J + 1)
        step = 2 * J + half + 3
        if step <= 7:
            rs_step(step)
        elif step == 8:
            collect()
        elif step <= 16:
            ag_step(step - 8)

    head()

    def block(I, J):
        return a_ref[I // 4, I % 4, :, :, :, lanes(J)].reshape(BS, BS)

    @pl.loop(0, NB)
    def _(Jd):
        for J in range(NB):
            @pl.when(Jd == J)
            def _(J=J):
                a3_wait(J)
                own = slice(BS * J, BS * J + BS)
                c = jnp.concatenate([block(I, J) for I in range(J, NB)], axis=0)
                if J > 0:
                    c = c - dot_nt(l_ref[BS * J:, :BS * J], l_ref[own, :BS * J])
                cbuf[:BS * (NB - J), :] = c
                tick(J, 0)
        factor_block(cbuf.at[0:BS], w_ref.at[Jd], 0, 8)
        for J in range(NB):
            @pl.when(Jd == J)
            def _(J=J):
                tick(J, 1)
        factor_block(cbuf.at[0:BS], w_ref.at[Jd], 8, 16)
        for J in range(NB):
            @pl.when(Jd == J)
            def _(J=J):
                own = slice(BS * J, BS * J + BS)
                l_ref[own, own] = cbuf[:BS, :].T
                if J < NB - 1:
                    low = slice(BS * (J + 1), NB * BS)
                    x = dot_nt(cbuf[BS:BS * (NB - J), :], w_ref[J])
                    l_ref[low, own] = x
                    lhi[low, own], llo[low, own] = split(x)

    start = pl.multiple_of(me_row * 32, 32)
    lane = lax.broadcasted_iota(jnp.int32, (32, NB * BS), 1)
    df_out[...] = jnp.where(lane < (me_row // 4 + 1) * BS, l_ref[pl.ds(start, 32), :], 0.0)
    b1_wait()
    hand_wait()
    for m in range(4):
        cs = slice(256 * m, 256 * m + 256)
        w0, w1 = w_ref[2 * m], w_ref[2 * m + 1]
        l10 = l_ref[256 * m + BS:256 * m + 256, 256 * m:256 * m + BS]
        w10 = -dot_nn(w1, dot_nn(l10, w0))
        wide = jnp.concatenate([
            jnp.concatenate([w0, jnp.zeros_like(w0)], axis=1),
            jnp.concatenate([w10, w1], axis=1)], axis=0)
        wh, wl = split(wide)
        for g in range(2):
            if g == 0:
                v = rp[:, :, :, :, cs].reshape(512, 256)
            else:
                v = cp[:, :, :, cs].reshape(512, 256)
            if m > 0:
                v = v - dot3(xhi[g, :, :256 * m], xlo[g, :, :256 * m],
                             lhi[cs, :256 * m], llo[cs, :256 * m])
            vh, vl = split(v)
            x = dot3(vh, vl, wh, wl)
            if g == 0:
                xs[m] = x
                xx(m).start()
            xhi[g, :, cs], xlo[g, :, cs] = split(x)

    def finish(g):
        t_copy(g).wait()
        slot = k if g == 0 else 1 - k
        live = tm_ref[2 * me_row + slot] >= me_col
        b = 2 * g
        prod = dot3(xhi[b], xlo[b], xhi[1], xlo[1])
        tbuf[g] = jnp.where(live, tbuf[g] - prod, 0.0)
        o_copy(g).start()

    finish(0)
    for m in range(4):
        cs = slice(256 * m, 256 * m + 256)
        xx(m).wait_recv()
        xhi[2, :, cs], xlo[2, :, cs] = split(xo[m])
    finish(1)
    mine = pl.ds(pl.multiple_of(me_col * 32, 32), 32)
    for m in range(4):
        cs = slice(256 * m, 256 * m + 256)
        own, other = xs[m, mine, :], xo[m, mine, :]
        pf_out[0, :, cs] = jnp.where(k == 0, own, other)
        pf_out[1, :, cs] = jnp.where(k == 0, other, own)
    sends_done()
    for g in range(2):
        o_copy(g).wait()


def per_device(trailing, panel_block, diag_block, tile_map):
    sem = pltpu.SemaphoreType.DMA
    vm = pl.BlockSpec(memory_space=pltpu.VMEM)
    updated, piece, diag = pl.pallas_call(
        kernel,
        out_shape=(
            jax.ShapeDtypeStruct((2, 512, 512), F32),
            jax.ShapeDtypeStruct((2, 32, 1024), F32),
            jax.ShapeDtypeStruct((32, 1024), F32),
        ),
        in_specs=[pl.BlockSpec(memory_space=pltpu.SMEM), vm, vm, pl.BlockSpec(memory_space=pl.ANY)],
        out_specs=(pl.BlockSpec(memory_space=pl.ANY), vm, vm),
        scratch_shapes=[
            pltpu.VMEM((2, 4, 4, 4, 8, 1024), F32),
            pltpu.VMEM((1024, 1024), F32),
            pltpu.VMEM((NB, BS, BS), F32),
            pltpu.VMEM((1024, BS), F32),
            pltpu.VMEM((2, 4, 2, 32, 1024), F32),
            pltpu.VMEM((16, 2, 16, 1024), F32),
            pltpu.VMEM((2, 2, 16, 1024), F32),
            pltpu.VMEM((9, 16, 1024), F32),
            pltpu.VMEM((8, 16, 1024), F32),
            pltpu.VMEM((16, 16, 1024), F32),
            pltpu.VMEM((4, 512, 256), F32),
            pltpu.VMEM((4, 512, 256), F32),
            pltpu.VMEM((3, 512, 1024), BF16),
            pltpu.VMEM((3, 512, 1024), BF16),
            pltpu.VMEM((1024, 1024), BF16),
            pltpu.VMEM((1024, 1024), BF16),
            pltpu.VMEM((2, 512, 512), F32),
            sem((2,)), sem((2,)), sem((5,)),
            sem((2, 16)), sem((2, 4)), sem((8, 16)), sem((8, 16)), sem((8, 2)), sem((8, 2)),
            sem((8, 2)), sem((16,)), sem((2, 8, 2)), sem((2, 8, 2)), sem((1,)), sem((1,)),
            sem((2, 8, 2)), sem((2, 8, 2)), sem((16, 2)), sem((16, 2)),
            sem((4,)), sem((4,)),
        ],
        compiler_params=pltpu.CompilerParams(
            collective_id=0, has_side_effects=True, vmem_limit_bytes=60 << 20
        ),
    )(tile_map, diag_block.reshape(4, 8, 1024), panel_block, trailing[:, 0])
    return (updated[:, None], piece, diag)


def solution(mesh):
    in_specs = (P("row", "col", None, None), P("row", "col", None), P("row", None), P())
    out_specs = (P("row", "col", None, None), P("row", "col", None), P("row", None))
    return jax.shard_map(
        per_device, mesh=mesh, in_specs=in_specs, out_specs=out_specs, check_vma=False
    )
```

```python
import jax
import jax.numpy as jnp
from jax import lax
from jax.experimental import pallas as pl
from jax.experimental.pallas import tpu as pltpu
from jax.sharding import PartitionSpec as P

F32 = jnp.float32
BF16 = jnp.bfloat16
MESH = pl.DeviceIdType.MESH
NB = 8
BS = 128


def dot_nt(a, b):
    return lax.dot_general(
        a, b, (((1,), (1,)), ((), ())),
        precision=lax.Precision.HIGHEST, preferred_element_type=F32,
    )


def dot_nn(a, b):
    return lax.dot_general(
        a, b, (((1,), (0,)), ((), ())),
        precision=lax.Precision.HIGHEST, preferred_element_type=F32,
    )


def split(x):
    hi = x.astype(BF16)
    return hi, (x - hi.astype(F32)).astype(BF16)


def dot3(ah, al, bh, bl):
    def one(a, b):
        return lax.dot_general(
            a, b, (((1,), (1,)), ((), ())), preferred_element_type=F32
        )
    return one(ah, bh) + (one(ah, bl) + one(al, bh))


def factor_block(d_ref, w_ref, begin, end):
    iota = lax.broadcasted_iota(jnp.int32, (8, BS), 0)
    lane = lax.broadcasted_iota(jnp.int32, (8, BS), 1)
    groups = BS // 8

    def row(x, j):
        return jnp.broadcast_to(x[j:j + 1, :], (8, BS))

    def column(x, j):
        return jnp.broadcast_to(x[:, j:j + 1], (8, BS))

    if begin == 0:
        for q in range(groups):
            w_ref[8 * q:8 * q + 8, :] = jnp.where(lane == iota + 8 * q, 1.0, 0.0).astype(F32)
    for p in range(begin, end):
        base = 8 * p
        rows = slice(base, base + 8)
        d = d_ref[rows, :]
        w = w_ref[rows, :]
        cols = [column(d, base + k) for k in range(8)]
        inverse, pivots, heads = [], [], []
        for j in range(8):
            pivot = row(cols[j], j)
            inv = 1.0 / pivot
            pivots.append(pivot)
            inverse.append(inv)
            below = jnp.where(iota > j, cols[j], 0.0)
            head = [None] * 8
            for k in range(j + 1, 8):
                head[k] = row(cols[k], j)
                cols[k] = cols[k] - (below * head[k]) * inv
            heads.append(head)
            m = below * inv
            d = d - m * row(d, j)
            w = w - m * row(w, j)
        d_rows = [row(d, j) for j in range(8)]
        w_rows = [row(w, j) for j in range(8)]
        diag = pivots[7]
        for j in range(7):
            diag = jnp.where(iota == j, pivots[j], diag)
        scale = lax.rsqrt(diag)
        d_ref[rows, :] = jnp.where(lane >= iota + base, d * scale, 0.0)
        w_ref[rows, :] = w * scale
        for q in range(p + 1, groups):
            part = slice(8 * q, 8 * q + 8)
            dq = d_ref[part, :]
            wq = w_ref[part, :]
            cq = [column(dq, base + k) for k in range(8)]
            for j in range(8):
                mq = cq[j] * inverse[j]
                for k in range(j + 1, 8):
                    cq[k] = cq[k] - mq * heads[j][k]
                dq = dq - mq * d_rows[j]
                wq = wq - mq * w_rows[j]
            d_ref[part, :] = dq
            w_ref[part, :] = wq


def kernel(
    tm_ref, a_in, b_in, t_hbm,
    out_hbm, pf_out, df_out,
    a_ref, l_ref, w_ref, cbuf, rp, cp, bx, rsp, rsm, items,
    xs, xo, xhi, xlo, lhi, llo, tbuf,
    t_sem, o_sem, loc, s1, r1, s2, r2, s3, r3, sb, rb, srs, rrs, sx, rx, sag, rag, sa, ra,
    sxx, rxx,
):
    me_row = lax.axis_index("row")
    me_col = lax.axis_index("col")
    h, z = me_row // 16, me_row % 16
    l, y, k = me_col // 8, (me_col // 2) % 4, me_col % 2
    zq, zr = z // 4, z % 4
    turn = 2 * k + l
    plane = h * 8 + l * 4 + y
    chip = l * 4 + y
    sib = me_col + 1 - 2 * k

    def remote(src, dst, ssem, rsem, row, col):
        return pltpu.make_async_remote_copy(
            src_ref=src, dst_ref=dst, send_sem=ssem, recv_sem=rsem,
            device_id={"row": row, "col": col}, device_id_type=MESH,
        )

    def greet(row, col):
        pl.semaphore_signal(
            pltpu.get_barrier_semaphore(), inc=1,
            device_id={"row": row, "col": col}, device_id_type=MESH,
        )

    @pl.loop(0, 15)
    def _(i):
        d = 8 + (i + 1) // 2 * (1 - 2 * (i % 2))
        greet(h * 16 + (z + d) % 16, me_col)

    @pl.loop(1, 32)
    def _(d):
        q = (h * 16 + me_col + d) % 32
        greet((q // 16) * 16 + z, q % 16)

    def t_copy(g):
        slot = k if g == 0 else 1 - k
        return pltpu.make_async_copy(t_hbm.at[slot], tbuf.at[g], t_sem.at[g])

    def o_copy(g):
        slot = k if g == 0 else 1 - k
        return pltpu.make_async_copy(tbuf.at[g], out_hbm.at[slot], o_sem.at[g])

    for s in range(2):
        t_copy(s).start()

    pl.semaphore_wait(pltpu.get_barrier_semaphore(), 46)

    def lanes(J):
        return slice(BS * J, BS * J + BS)

    pieces = (slice(0, BS), slice(BS, NB * BS))

    def a1(n, d):
        return remote(a_in.at[y, :, pieces[n]], a_ref.at[h, zq, zr, y, :, pieces[n]],
                      s1.at[n, d], r1.at[n, zq], h * 16 + (z + d) % 16, me_col)

    def a_local(n):
        return pltpu.make_async_copy(
            a_in.at[y, :, pieces[n]], a_ref.at[h, zq, zr, y, :, pieces[n]], loc.at[n])

    def a1_start(n):
        @pl.when(zr == turn)
        def _():
            a_local(n).start()

            @pl.loop(0, 15)
            def _(i):
                a1(n, 8 + (i + 1) // 2 * (1 - 2 * (i % 2))).start()

    def a1_wait(n):
        @pl.loop(0, 4)
        def _(q):
            @pl.when(q * 4 + turn != z)
            def _():
                sl = a_ref.at[h, q, turn, y, :, pieces[n]]
                pltpu.make_async_copy(sl, sl, r1.at[n, q]).wait()

        @pl.when(zr == turn)
        def _():
            a_local(n).wait()

    def first(J, hh):
        return min(max(J - 4 * hh, 0), 4)

    def a2(J, hh, d):
        q = (plane + d) % 16
        sl = a_ref.at[hh, first(J, hh):4, turn, y, :, lanes(J)]
        return remote(sl, sl, s2.at[J, d], r2.at[J, plane],
                      (q // 8) * 16 + z, (q % 8) * 2 + k)

    def a2_each(J, act):
        for hh in range(2):
            if first(J, hh) < 4:
                @pl.when(h == hh)
                def _(hh=hh):
                    @pl.loop(1, 16)
                    def _(d):
                        act(a2(J, hh, d))

    def a2_start(J):
        a2_each(J, lambda c: c.start())

    def a2_sent(J):
        a2_each(J, lambda c: c.wait_send())

    def a2_wait(J):
        for hh in range(2):
            if first(J, hh) < 4:
                @pl.loop(0, 8)
                def _(c, hh=hh):
                    @pl.when(hh * 8 + c != plane)
                    def _():
                        sl = a_ref.at[hh, first(J, hh):4, 2 * k + c // 4, c % 4, :, lanes(J)]
                        pltpu.make_async_copy(sl, sl, r2.at[J, hh * 8 + c]).wait()

    def a3(J, hh, kk):
        sl = a_ref.at[hh, first(J, hh):4, pl.ds(2 * kk, 2), :, :, lanes(J)]
        return remote(sl, sl, s3.at[J, hh], r3.at[J, hh], me_row, sib)

    def halves(J):
        return [hh for hh in range(2) if first(J, hh) < 4]

    def a3_start(J):
        for hh in halves(J):
            a3(J, hh, k).start()

    def a3_wait(J):
        for hh in halves(J):
            a3(J, hh, 1 - k).wait_recv()

    def a3_sent(J):
        for hh in halves(J):
            a3(J, hh, k).wait_send()

    def b1(d, s):
        q = (chip + d) % 8
        return remote(b_in.at[s], rp.at[l, y, k], sb.at[d, s], rb.at[me_col],
                      me_row, q * 2 + s)

    def b_local():
        return pltpu.make_async_copy(b_in.at[k], rp.at[l, y, k], loc.at[2])

    def b1_each(act):
        for s in range(2):
            @pl.when(s != k)
            def _(s=s):
                act(b1(0, s))

            @pl.loop(1, 8)
            def _(d, s=s):
                act(b1(d, s))

    def b1_start():
        b_local().start()
        b1_each(lambda c: c.start())

    def b1_wait():
        b_local().wait()

        @pl.loop(0, 16)
        def _(c):
            @pl.when(c != me_col)
            def _():
                sl = rp.at[c // 8, (c // 2) % 4, c % 2]
                pltpu.make_async_copy(sl, sl, rb.at[c]).wait()

    right = h * 16 + (z + 1) % 16
    left = h * 16 + (z + 15) % 16
    NS = 2
    HR = 16
    ids = [tm_ref[2 * z], tm_ref[2 * z + 1], tm_ref[2 * z + 32], tm_ref[2 * z + 33]]

    def part(n):
        return pl.ds(n * (HR // NS), HR // NS)

    def swap():
        return remote(b_in.at[:, pl.ds((1 - h) * HR, HR)], bx.at[h], sx.at[0], rx.at[0],
                      (1 - h) * 16 + z, me_col)

    def swap_local():
        return pltpu.make_async_copy(b_in.at[:, pl.ds(h * HR, HR)], bx.at[h], loc.at[3])

    def swap_start():
        swap().start()
        swap_local().start()

    def swap_wait():
        swap_local().wait()
        sl = bx.at[1 - h]
        pltpu.make_async_copy(sl, sl, rx.at[0]).wait()

    def pick(item, n, value):
        for i in range(4):
            value = jnp.where(ids[i] == item, bx[i // 2, i % 2, part(n), :], value)
        return value

    def rs(way, t, n):
        buf = rsm if way else rsp
        return remote(buf.at[t, part(n)], buf.at[t + 1, part(n)],
                      srs.at[way, t, n], rrs.at[way, t, n], left if way else right, me_col)

    def rs_step(t):
        for n in range(NS):
            for way in range(2):
                if t < 8 - way:
                    buf = rsm if way else rsp
                    item = (z + 9 + t) % 16 if way else (z + 8 - t + 16) % 16
                    if t > 0:
                        rs(way, t - 1, n).wait_recv()
                        came = buf[t, part(n), :]
                    else:
                        came = bx[0, 0, part(n), :]
                    buf[t, part(n), :] = pick(item, n, came)
                    rs(way, t, n).start()

    def owner_of(item):
        def look(i, best):
            return jnp.where(tm_ref[i] == item, i, best)
        return lax.fori_loop(0, 64, look, jnp.int32(0))

    def ag_on(way, kind, t):
        return not (way == 1 and kind == 0 and t == 3)

    def ag(way, kind, t):
        item = (z + 2 * t) % 16 if way else (z - 2 * t + 16) % 16
        far = 2 - kind
        to = (z + 16 - far) % 16 if way else (z + far) % 16
        return remote(items.at[item], items.at[item], sag.at[way, kind, t],
                      rag.at[way, kind, t], h * 16 + to, me_col)

    def ag_start(t):
        for kind in range(2):
            for way in range(2):
                if ag_on(way, kind, t):
                    ag(way, kind, t).start()

    def ag_item(way, kind, t):
        far = 2 - kind + 2 * t
        return (z + far) % 16 if way else (z - far + 16) % 16

    def ag_wait(way, kind, t):
        sl = items.at[ag_item(way, kind, t)]
        pltpu.make_async_copy(sl, sl, rag.at[way, kind, t]).wait()

    def hand(item, hh):
        return remote(items.at[item], cp.at[me_col, h], sa.at[item, hh], ra.at[me_col, h],
                      hh * 16 + z, item)

    def hand_local():
        return pltpu.make_async_copy(items.at[me_col], cp.at[me_col, h], loc.at[4])

    def hand_each(item, act, act_local):
        if act_local is not None:
            @pl.when(item == me_col)
            def _():
                act_local(hand_local())

        @pl.when(item != me_col)
        def _():
            act(hand(item, h))
        act(hand(item, 1 - h))

    def hand_start(item):
        hand_each(item, lambda c: c.start(), lambda c: c.start())

    def collect():
        slot = owner_of(z)
        gap = ((slot // 2) % 16 - z + 16) % 16
        for n in range(NS):
            rs(0, 7, n).wait_recv()
            rs(1, 6, n).wait_recv()
            chain = jnp.where(gap >= 8, rsp[8, part(n), :], rsm[7, part(n), :])
            items[z, part(n), :] = pick(z, n, chain)
        ag_start(0)
        hand_start(z)

    def ag_step(t):
        arrived = [(way, kind) for kind in range(2) for way in range(2)
                   if ag_on(way, kind, t - 1)]
        for way, kind in arrived:
            if kind == 0:
                ag_wait(way, kind, t - 1)
        if t < 4:
            ag_start(t)
        for way, kind in arrived:
            if kind == 1:
                ag_wait(way, kind, t - 1)
        for way, kind in arrived:
            hand_start(ag_item(way, kind, t - 1))

    def hand_wait():
        hand_local().wait()
        for hh in range(2):
            @pl.loop(0, 16)
            def _(c, hh=hh):
                @pl.when((c != me_col) | (h != hh))
                def _():
                    pltpu.make_async_copy(cp.at[c, hh], cp.at[c, hh], ra.at[c, hh]).wait()

    def xx(m):
        return remote(xs.at[m], xo.at[m], sxx.at[m], rxx.at[m], me_row, sib)

    def sends_done():
        @pl.when(zr == turn)
        def _():
            for n in range(2):
                @pl.loop(1, 16)
                def _(d, n=n):
                    a1(n, d).wait_send()
        for J in range(NB):
            a2_sent(J)
            a3_sent(J)
        b1_each(lambda c: c.wait_send())
        swap().wait_send()
        for n in range(NS):
            for way in range(2):
                for t in range(8 - way):
                    rs(way, t, n).wait_send()
        for t in range(4):
            for kind in range(2):
                for way in range(2):
                    if ag_on(way, kind, t):
                        ag(way, kind, t).wait_send()

        @pl.loop(0, 16)
        def _(c):
            hand_each(c, lambda q: q.wait_send(), None)
        for m in range(4):
            xx(m).wait_send()

    def head():
        a1_start(0)
        swap_start()
        a1_start(1)
        swap_wait()
        rs_step(0)
        a1_wait(0)
        a2_start(0)
        rs_step(1)
        a1_wait(1)
        for J in range(1, 4):
            a2_start(J)
        rs_step(2)
        a2_wait(0)
        a3_start(0)
        for J in range(4, NB):
            a2_start(J)
        b1_start()
        rs_step(3)

    def tick(J, half):
        if half == 1 and J < NB - 1:
            a2_wait(J + 1)
            a3_start(J + 1)
        step = 2 * J + half + 3
        if 4 <= step <= 7:
            rs_step(step)
        elif step == 8:
            collect()
        elif half == 1 and 3 <= J <= 6:
            ag_step(J - 2)

    head()

    def block(I, J):
        return a_ref[I // 4, I % 4, :, :, :, lanes(J)].reshape(BS, BS)

    @pl.loop(0, NB)
    def _(Jd):
        for J in range(NB):
            @pl.when(Jd == J)
            def _(J=J):
                a3_wait(J)
                own = slice(BS * J, BS * J + BS)
                c = jnp.concatenate([block(I, J) for I in range(J, NB)], axis=0)
                if J > 0:
                    c = c - dot_nt(l_ref[BS * J:, :BS * J], l_ref[own, :BS * J])
                cbuf[:BS * (NB - J), :] = c
                tick(J, 0)
        factor_block(cbuf.at[0:BS], w_ref.at[Jd], 0, 8)
        for J in range(NB):
            @pl.when(Jd == J)
            def _(J=J):
                tick(J, 1)
        factor_block(cbuf.at[0:BS], w_ref.at[Jd], 8, 16)
        for J in range(NB):
            @pl.when(Jd == J)
            def _(J=J):
                own = slice(BS * J, BS * J + BS)
                l_ref[own, own] = cbuf[:BS, :].T
                if J < NB - 1:
                    low = slice(BS * (J + 1), NB * BS)
                    x = dot_nt(cbuf[BS:BS * (NB - J), :], w_ref[J])
                    l_ref[low, own] = x
                    lhi[low, own], llo[low, own] = split(x)

    start = pl.multiple_of(me_row * 32, 32)
    lane = lax.broadcasted_iota(jnp.int32, (32, NB * BS), 1)
    df_out[...] = jnp.where(lane < (me_row // 4 + 1) * BS, l_ref[pl.ds(start, 32), :], 0.0)
    b1_wait()
    hand_wait()
    for m in range(4):
        cs = slice(256 * m, 256 * m + 256)
        w0, w1 = w_ref[2 * m], w_ref[2 * m + 1]
        l10 = l_ref[256 * m + BS:256 * m + 256, 256 * m:256 * m + BS]
        w10 = -dot_nn(w1, dot_nn(l10, w0))
        wide = jnp.concatenate([
            jnp.concatenate([w0, jnp.zeros_like(w0)], axis=1),
            jnp.concatenate([w10, w1], axis=1)], axis=0)
        wh, wl = split(wide)
        for g in range(2):
            if g == 0:
                v = rp[:, :, :, :, cs].reshape(512, 256)
            else:
                v = cp[:, :, :, cs].reshape(512, 256)
            if m > 0:
                v = v - dot3(xhi[g, :, :256 * m], xlo[g, :, :256 * m],
                             lhi[cs, :256 * m], llo[cs, :256 * m])
            vh, vl = split(v)
            x = dot3(vh, vl, wh, wl)
            if g == 0:
                xs[m] = x
                xx(m).start()
            xhi[g, :, cs], xlo[g, :, cs] = split(x)

    def finish(g):
        t_copy(g).wait()
        slot = k if g == 0 else 1 - k
        live = tm_ref[2 * me_row + slot] >= me_col
        b = 2 * g
        prod = dot3(xhi[b], xlo[b], xhi[1], xlo[1])
        tbuf[g] = jnp.where(live, tbuf[g] - prod, 0.0)
        o_copy(g).start()

    finish(0)
    for m in range(4):
        cs = slice(256 * m, 256 * m + 256)
        xx(m).wait_recv()
        xhi[2, :, cs], xlo[2, :, cs] = split(xo[m])
    finish(1)
    mine = pl.ds(pl.multiple_of(me_col * 32, 32), 32)
    for m in range(4):
        cs = slice(256 * m, 256 * m + 256)
        own, other = xs[m, mine, :], xo[m, mine, :]
        pf_out[0, :, cs] = jnp.where(k == 0, own, other)
        pf_out[1, :, cs] = jnp.where(k == 0, other, own)
    sends_done()
    for g in range(2):
        o_copy(g).wait()


def per_device(trailing, panel_block, diag_block, tile_map):
    sem = pltpu.SemaphoreType.DMA
    vm = pl.BlockSpec(memory_space=pltpu.VMEM)
    updated, piece, diag = pl.pallas_call(
        kernel,
        out_shape=(
            jax.ShapeDtypeStruct((2, 512, 512), F32),
            jax.ShapeDtypeStruct((2, 32, 1024), F32),
            jax.ShapeDtypeStruct((32, 1024), F32),
        ),
        in_specs=[pl.BlockSpec(memory_space=pltpu.SMEM), vm, vm, pl.BlockSpec(memory_space=pl.ANY)],
        out_specs=(pl.BlockSpec(memory_space=pl.ANY), vm, vm),
        scratch_shapes=[
            pltpu.VMEM((2, 4, 4, 4, 8, 1024), F32),
            pltpu.VMEM((1024, 1024), F32),
            pltpu.VMEM((NB, BS, BS), F32),
            pltpu.VMEM((1024, BS), F32),
            pltpu.VMEM((2, 4, 2, 32, 1024), F32),
            pltpu.VMEM((16, 2, 16, 1024), F32),
            pltpu.VMEM((2, 2, 16, 1024), F32),
            pltpu.VMEM((9, 16, 1024), F32),
            pltpu.VMEM((8, 16, 1024), F32),
            pltpu.VMEM((16, 16, 1024), F32),
            pltpu.VMEM((4, 512, 256), F32),
            pltpu.VMEM((4, 512, 256), F32),
            pltpu.VMEM((3, 512, 1024), BF16),
            pltpu.VMEM((3, 512, 1024), BF16),
            pltpu.VMEM((1024, 1024), BF16),
            pltpu.VMEM((1024, 1024), BF16),
            pltpu.VMEM((2, 512, 512), F32),
            sem((2,)), sem((2,)), sem((5,)),
            sem((2, 16)), sem((2, 4)), sem((8, 16)), sem((8, 16)), sem((8, 2)), sem((8, 2)),
            sem((8, 2)), sem((16,)), sem((2, 8, 2)), sem((2, 8, 2)), sem((1,)), sem((1,)),
            sem((2, 2, 4)), sem((2, 2, 4)), sem((16, 2)), sem((16, 2)),
            sem((4,)), sem((4,)),
        ],
        compiler_params=pltpu.CompilerParams(
            collective_id=0, has_side_effects=True, vmem_limit_bytes=60 << 20
        ),
    )(tile_map, diag_block.reshape(4, 8, 1024), panel_block, trailing[:, 0])
    return (updated[:, None], piece, diag)


def solution(mesh):
    in_specs = (P("row", "col", None, None), P("row", "col", None), P("row", None), P())
    out_specs = (P("row", "col", None, None), P("row", "col", None), P("row", None))
    return jax.shard_map(
        per_device, mesh=mesh, in_specs=in_specs, out_specs=out_specs, check_vma=False
    )
```

```python
import jax
import jax.numpy as jnp
from jax import lax
from jax.experimental import pallas as pl
from jax.experimental.pallas import tpu as pltpu
from jax.sharding import PartitionSpec as P

F32 = jnp.float32
BF16 = jnp.bfloat16
MESH = pl.DeviceIdType.MESH
NB = 8
BS = 128


def dot_nt(a, b):
    return lax.dot_general(
        a, b, (((1,), (1,)), ((), ())),
        precision=lax.Precision.HIGHEST, preferred_element_type=F32,
    )


def dot_nn(a, b):
    return lax.dot_general(
        a, b, (((1,), (0,)), ((), ())),
        precision=lax.Precision.HIGHEST, preferred_element_type=F32,
    )


def split(x):
    hi = x.astype(BF16)
    return hi, (x - hi.astype(F32)).astype(BF16)


def dot3(ah, al, bh, bl):
    def one(a, b):
        return lax.dot_general(
            a, b, (((1,), (1,)), ((), ())), preferred_element_type=F32
        )
    return one(ah, bh) + (one(ah, bl) + one(al, bh))


def factor_block(d_ref, w_ref, begin, end):
    iota = lax.broadcasted_iota(jnp.int32, (8, BS), 0)
    lane = lax.broadcasted_iota(jnp.int32, (8, BS), 1)
    groups = BS // 8

    def row(x, j):
        return jnp.broadcast_to(x[j:j + 1, :], (8, BS))

    def column(x, j):
        return jnp.broadcast_to(x[:, j:j + 1], (8, BS))

    if begin == 0:
        for q in range(groups):
            w_ref[8 * q:8 * q + 8, :] = jnp.where(lane == iota + 8 * q, 1.0, 0.0).astype(F32)
    for p in range(begin, end):
        base = 8 * p
        rows = slice(base, base + 8)
        d = d_ref[rows, :]
        w = w_ref[rows, :]
        cols = [column(d, base + k) for k in range(8)]
        inverse, pivots, heads = [], [], []
        for j in range(8):
            pivot = row(cols[j], j)
            inv = 1.0 / pivot
            pivots.append(pivot)
            inverse.append(inv)
            below = jnp.where(iota > j, cols[j], 0.0)
            head = [None] * 8
            for k in range(j + 1, 8):
                head[k] = row(cols[k], j)
                cols[k] = cols[k] - (below * head[k]) * inv
            heads.append(head)
            m = below * inv
            d = d - m * row(d, j)
            w = w - m * row(w, j)
        d_rows = [row(d, j) for j in range(8)]
        w_rows = [row(w, j) for j in range(8)]
        diag = pivots[7]
        for j in range(7):
            diag = jnp.where(iota == j, pivots[j], diag)
        scale = lax.rsqrt(diag)
        d_ref[rows, :] = jnp.where(lane >= iota + base, d * scale, 0.0)
        w_ref[rows, :] = w * scale
        for q in range(p + 1, groups):
            part = slice(8 * q, 8 * q + 8)
            dq = d_ref[part, :]
            wq = w_ref[part, :]
            cq = [column(dq, base + k) for k in range(8)]
            for j in range(8):
                mq = cq[j] * inverse[j]
                for k in range(j + 1, 8):
                    cq[k] = cq[k] - mq * heads[j][k]
                dq = dq - mq * d_rows[j]
                wq = wq - mq * w_rows[j]
            d_ref[part, :] = dq
            w_ref[part, :] = wq


def kernel(
    tm_ref, a_in, b_in, t_hbm,
    out_hbm, pf_out, df_out,
    a_ref, l_ref, w_ref, cbuf, rp, cp, bx, rsp, rsm, items,
    xs, xo, xhi, xlo, lhi, llo, tbuf,
    t_sem, o_sem, loc, s1, r1, s2, r2, s3, r3, sb, rb, srs, rrs, sx, rx, sag, rag, sa, ra,
    sxx, rxx,
):
    me_row = lax.axis_index("row")
    me_col = lax.axis_index("col")
    h, z = me_row // 16, me_row % 16
    l, y, k = me_col // 8, (me_col // 2) % 4, me_col % 2
    zq, zr = z // 4, z % 4
    turn = 2 * k + l
    plane = h * 8 + l * 4 + y
    chip = l * 4 + y
    sib = me_col + 1 - 2 * k

    def remote(src, dst, ssem, rsem, row, col):
        return pltpu.make_async_remote_copy(
            src_ref=src, dst_ref=dst, send_sem=ssem, recv_sem=rsem,
            device_id={"row": row, "col": col}, device_id_type=MESH,
        )

    def greet(row, col):
        pl.semaphore_signal(
            pltpu.get_barrier_semaphore(), inc=1,
            device_id={"row": row, "col": col}, device_id_type=MESH,
        )

    @pl.loop(0, 15)
    def _(i):
        d = 8 + (i + 1) // 2 * (1 - 2 * (i % 2))
        greet(h * 16 + (z + d) % 16, me_col)

    @pl.loop(1, 32)
    def _(d):
        q = (h * 16 + me_col + d) % 32
        greet((q // 16) * 16 + z, q % 16)

    def t_copy(g):
        slot = k if g == 0 else 1 - k
        return pltpu.make_async_copy(t_hbm.at[slot], tbuf.at[g], t_sem.at[g])

    def o_copy(g):
        slot = k if g == 0 else 1 - k
        return pltpu.make_async_copy(tbuf.at[g], out_hbm.at[slot], o_sem.at[g])

    for s in range(2):
        t_copy(s).start()

    pl.semaphore_wait(pltpu.get_barrier_semaphore(), 46)

    def lanes(J):
        return slice(BS * J, BS * J + BS)

    pieces = (slice(0, BS), slice(BS, NB * BS))

    def a1(n, d):
        return remote(a_in.at[y, :, pieces[n]], a_ref.at[h, zq, zr, y, :, pieces[n]],
                      s1.at[n, d], r1.at[n, zq], h * 16 + (z + d) % 16, me_col)

    def a_local(n):
        return pltpu.make_async_copy(
            a_in.at[y, :, pieces[n]], a_ref.at[h, zq, zr, y, :, pieces[n]], loc.at[n])

    def a1_start(n):
        @pl.when(zr == turn)
        def _():
            a_local(n).start()

            @pl.loop(0, 15)
            def _(i):
                a1(n, 8 + (i + 1) // 2 * (1 - 2 * (i % 2))).start()

    def a1_wait(n):
        @pl.loop(0, 4)
        def _(q):
            @pl.when(q * 4 + turn != z)
            def _():
                sl = a_ref.at[h, q, turn, y, :, pieces[n]]
                pltpu.make_async_copy(sl, sl, r1.at[n, q]).wait()

        @pl.when(zr == turn)
        def _():
            a_local(n).wait()

    def first(J, hh):
        return min(max(J - 4 * hh, 0), 4)

    def a2(J, hh, d):
        q = (plane + d) % 16
        sl = a_ref.at[hh, first(J, hh):4, turn, y, :, lanes(J)]
        return remote(sl, sl, s2.at[J, d], r2.at[J, plane],
                      (q // 8) * 16 + z, (q % 8) * 2 + k)

    def a2_each(J, act):
        for hh in range(2):
            if first(J, hh) < 4:
                @pl.when(h == hh)
                def _(hh=hh):
                    @pl.loop(1, 16)
                    def _(d):
                        act(a2(J, hh, d))

    def a2_start(J):
        a2_each(J, lambda c: c.start())

    def a2_sent(J):
        a2_each(J, lambda c: c.wait_send())

    def a2_wait(J):
        for hh in range(2):
            if first(J, hh) < 4:
                @pl.loop(0, 8)
                def _(c, hh=hh):
                    @pl.when(hh * 8 + c != plane)
                    def _():
                        sl = a_ref.at[hh, first(J, hh):4, 2 * k + c // 4, c % 4, :, lanes(J)]
                        pltpu.make_async_copy(sl, sl, r2.at[J, hh * 8 + c]).wait()

    def a3(J, hh, kk):
        sl = a_ref.at[hh, first(J, hh):4, pl.ds(2 * kk, 2), :, :, lanes(J)]
        return remote(sl, sl, s3.at[J, hh], r3.at[J, hh], me_row, sib)

    def halves(J):
        return [hh for hh in range(2) if first(J, hh) < 4]

    def a3_start(J):
        for hh in halves(J):
            a3(J, hh, k).start()

    def a3_wait(J):
        for hh in halves(J):
            a3(J, hh, 1 - k).wait_recv()

    def a3_sent(J):
        for hh in halves(J):
            a3(J, hh, k).wait_send()

    def b1(d, s):
        q = (chip + d) % 8
        return remote(b_in.at[s], rp.at[l, y, k], sb.at[d, s], rb.at[me_col],
                      me_row, q * 2 + s)

    def b_local():
        return pltpu.make_async_copy(b_in.at[k], rp.at[l, y, k], loc.at[2])

    def b1_each(act):
        for s in range(2):
            @pl.when(s != k)
            def _(s=s):
                act(b1(0, s))

            @pl.loop(1, 8)
            def _(d, s=s):
                act(b1(d, s))

    def b1_start():
        b_local().start()
        b1_each(lambda c: c.start())

    def b1_wait():
        b_local().wait()

        @pl.loop(0, 16)
        def _(c):
            @pl.when(c != me_col)
            def _():
                sl = rp.at[c // 8, (c // 2) % 4, c % 2]
                pltpu.make_async_copy(sl, sl, rb.at[c]).wait()

    v = (z + 16 - me_col) % 16
    right = h * 16 + (z + 1) % 16
    left = h * 16 + (z + 15) % 16
    NS = 2
    HR = 16
    ids = [tm_ref[2 * z], tm_ref[2 * z + 1], tm_ref[2 * z + 32], tm_ref[2 * z + 33]]

    def part(n):
        return pl.ds(n * (HR // NS), HR // NS)

    def swap():
        return remote(b_in.at[:, pl.ds((1 - h) * HR, HR)], bx.at[h], sx.at[0], rx.at[0],
                      (1 - h) * 16 + z, me_col)

    def swap_local():
        return pltpu.make_async_copy(b_in.at[:, pl.ds(h * HR, HR)], bx.at[h], loc.at[3])

    def swap_start():
        swap().start()
        swap_local().start()

    def swap_wait():
        swap_local().wait()
        sl = bx.at[1 - h]
        pltpu.make_async_copy(sl, sl, rx.at[0]).wait()

    def pick(item, n, value):
        for i in range(4):
            value = jnp.where(ids[i] == item, bx[i // 2, i % 2, part(n), :], value)
        return value

    def rs(way, t, n):
        buf = rsm if way else rsp
        return remote(buf.at[t, part(n)], buf.at[t + 1, part(n)],
                      srs.at[way, t, n], rrs.at[way, t, n], left if way else right, me_col)

    def rs_step(t):
        for n in range(NS):
            for way in range(2):
                if t < 8 - way:
                    buf = rsm if way else rsp
                    item = (v + 9 + t) % 16 if way else (v + 8 - t + 16) % 16
                    if t > 0:
                        rs(way, t - 1, n).wait_recv()
                        came = buf[t, part(n), :]
                    else:
                        came = bx[0, 0, part(n), :]
                    buf[t, part(n), :] = pick(item, n, came)
                    rs(way, t, n).start()

    def owner_of(item):
        def look(i, best):
            return jnp.where(tm_ref[i] == item, i, best)
        return lax.fori_loop(0, 64, look, jnp.int32(0))

    def ag_on(way, kind, t):
        return not (way == 1 and kind == 0 and t == 3)

    def ag(way, kind, t):
        item = (v + 2 * t) % 16 if way else (v - 2 * t + 16) % 16
        far = 2 - kind
        to = (z + 16 - far) % 16 if way else (z + far) % 16
        return remote(items.at[item], items.at[item], sag.at[way, kind, t],
                      rag.at[way, kind, t], h * 16 + to, me_col)

    def ag_start(t):
        for kind in range(2):
            for way in range(2):
                if ag_on(way, kind, t):
                    ag(way, kind, t).start()

    def ag_item(way, kind, t):
        far = 2 - kind + 2 * t
        return (v + far) % 16 if way else (v - far + 16) % 16

    def ag_wait(way, kind, t):
        sl = items.at[ag_item(way, kind, t)]
        pltpu.make_async_copy(sl, sl, rag.at[way, kind, t]).wait()

    def hand(item, hh):
        return remote(items.at[item], cp.at[me_col, h], sa.at[item, hh], ra.at[me_col, h],
                      hh * 16 + z, item)

    def hand_local():
        return pltpu.make_async_copy(items.at[me_col], cp.at[me_col, h], loc.at[4])

    def hand_each(item, act, act_local):
        if act_local is not None:
            @pl.when(item == me_col)
            def _():
                act_local(hand_local())

        @pl.when(item != me_col)
        def _():
            act(hand(item, h))
        act(hand(item, 1 - h))

    def hand_start(item):
        hand_each(item, lambda c: c.start(), lambda c: c.start())

    def collect():
        slot = owner_of(v)
        gap = ((slot // 2) % 16 - z + 16) % 16
        for n in range(NS):
            rs(0, 7, n).wait_recv()
            rs(1, 6, n).wait_recv()
            chain = jnp.where(gap >= 8, rsp[8, part(n), :], rsm[7, part(n), :])
            items[v, part(n), :] = pick(v, n, chain)
        ag_start(0)
        hand_start(v)

    def ag_step(t):
        arrived = [(way, kind) for kind in range(2) for way in range(2)
                   if ag_on(way, kind, t - 1)]
        for way, kind in arrived:
            if kind == 0:
                ag_wait(way, kind, t - 1)
        if t < 4:
            ag_start(t)
        for way, kind in arrived:
            if kind == 1:
                ag_wait(way, kind, t - 1)
        for way, kind in arrived:
            hand_start(ag_item(way, kind, t - 1))

    def hand_wait():
        hand_local().wait()
        for hh in range(2):
            @pl.loop(0, 16)
            def _(c, hh=hh):
                @pl.when((c != me_col) | (h != hh))
                def _():
                    pltpu.make_async_copy(cp.at[c, hh], cp.at[c, hh], ra.at[c, hh]).wait()

    def xx(m):
        return remote(xs.at[m], xo.at[m], sxx.at[m], rxx.at[m], me_row, sib)

    def sends_done():
        @pl.when(zr == turn)
        def _():
            for n in range(2):
                @pl.loop(1, 16)
                def _(d, n=n):
                    a1(n, d).wait_send()
        for J in range(NB):
            a2_sent(J)
            a3_sent(J)
        b1_each(lambda c: c.wait_send())
        swap().wait_send()
        for n in range(NS):
            for way in range(2):
                for t in range(8 - way):
                    rs(way, t, n).wait_send()
        for t in range(4):
            for kind in range(2):
                for way in range(2):
                    if ag_on(way, kind, t):
                        ag(way, kind, t).wait_send()

        @pl.loop(0, 16)
        def _(c):
            hand_each(c, lambda q: q.wait_send(), None)
        for m in range(4):
            xx(m).wait_send()

    def head():
        a1_start(0)
        swap_start()
        a1_start(1)
        swap_wait()
        rs_step(0)
        a1_wait(0)
        a2_start(0)
        rs_step(1)
        a1_wait(1)
        for J in range(1, 4):
            a2_start(J)
        rs_step(2)
        a2_wait(0)
        a3_start(0)
        for J in range(4, NB):
            a2_start(J)
        b1_start()
        rs_step(3)

    def tick(J, half):
        if half == 1 and J < NB - 1:
            a2_wait(J + 1)
            a3_start(J + 1)
        step = 2 * J + half + 3
        if 4 <= step <= 7:
            rs_step(step)
        elif step == 8:
            collect()
        elif half == 1 and 3 <= J <= 6:
            ag_step(J - 2)

    head()

    def block(I, J):
        return a_ref[I // 4, I % 4, :, :, :, lanes(J)].reshape(BS, BS)

    @pl.loop(0, NB)
    def _(Jd):
        for J in range(NB):
            @pl.when(Jd == J)
            def _(J=J):
                a3_wait(J)
                own = slice(BS * J, BS * J + BS)
                c = jnp.concatenate([block(I, J) for I in range(J, NB)], axis=0)
                if J > 0:
                    c = c - dot_nt(l_ref[BS * J:, :BS * J], l_ref[own, :BS * J])
                cbuf[:BS * (NB - J), :] = c
                tick(J, 0)
        factor_block(cbuf.at[0:BS], w_ref.at[Jd], 0, 8)
        for J in range(NB):
            @pl.when(Jd == J)
            def _(J=J):
                tick(J, 1)
        factor_block(cbuf.at[0:BS], w_ref.at[Jd], 8, 16)
        for J in range(NB):
            @pl.when(Jd == J)
            def _(J=J):
                own = slice(BS * J, BS * J + BS)
                l_ref[own, own] = cbuf[:BS, :].T
                if J < NB - 1:
                    low = slice(BS * (J + 1), NB * BS)
                    x = dot_nt(cbuf[BS:BS * (NB - J), :], w_ref[J])
                    l_ref[low, own] = x
                    lhi[low, own], llo[low, own] = split(x)

    start = pl.multiple_of(me_row * 32, 32)
    lane = lax.broadcasted_iota(jnp.int32, (32, NB * BS), 1)
    df_out[...] = jnp.where(lane < (me_row // 4 + 1) * BS, l_ref[pl.ds(start, 32), :], 0.0)
    b1_wait()
    hand_wait()
    for m in range(4):
        cs = slice(256 * m, 256 * m + 256)
        w0, w1 = w_ref[2 * m], w_ref[2 * m + 1]
        l10 = l_ref[256 * m + BS:256 * m + 256, 256 * m:256 * m + BS]
        w10 = -dot_nn(w1, dot_nn(l10, w0))
        wide = jnp.concatenate([
            jnp.concatenate([w0, jnp.zeros_like(w0)], axis=1),
            jnp.concatenate([w10, w1], axis=1)], axis=0)
        wh, wl = split(wide)
        for g in range(2):
            if g == 0:
                rows = rp[:, :, :, :, cs].reshape(512, 256)
            else:
                rows = cp[:, :, :, cs].reshape(512, 256)
            if m > 0:
                rows = rows - dot3(xhi[g, :, :256 * m], xlo[g, :, :256 * m],
                             lhi[cs, :256 * m], llo[cs, :256 * m])
            vh, vl = split(rows)
            x = dot3(vh, vl, wh, wl)
            if g == 0:
                xs[m] = x
                xx(m).start()
            xhi[g, :, cs], xlo[g, :, cs] = split(x)

    def finish(g):
        t_copy(g).wait()
        slot = k if g == 0 else 1 - k
        live = tm_ref[2 * me_row + slot] >= me_col
        b = 2 * g
        prod = dot3(xhi[b], xlo[b], xhi[1], xlo[1])
        tbuf[g] = jnp.where(live, tbuf[g] - prod, 0.0)
        o_copy(g).start()

    finish(0)
    for m in range(4):
        cs = slice(256 * m, 256 * m + 256)
        xx(m).wait_recv()
        xhi[2, :, cs], xlo[2, :, cs] = split(xo[m])
    finish(1)
    mine = pl.ds(pl.multiple_of(me_col * 32, 32), 32)
    for m in range(4):
        cs = slice(256 * m, 256 * m + 256)
        own, other = xs[m, mine, :], xo[m, mine, :]
        pf_out[0, :, cs] = jnp.where(k == 0, own, other)
        pf_out[1, :, cs] = jnp.where(k == 0, other, own)
    sends_done()
    for g in range(2):
        o_copy(g).wait()


def per_device(trailing, panel_block, diag_block, tile_map):
    sem = pltpu.SemaphoreType.DMA
    vm = pl.BlockSpec(memory_space=pltpu.VMEM)
    updated, piece, diag = pl.pallas_call(
        kernel,
        out_shape=(
            jax.ShapeDtypeStruct((2, 512, 512), F32),
            jax.ShapeDtypeStruct((2, 32, 1024), F32),
            jax.ShapeDtypeStruct((32, 1024), F32),
        ),
        in_specs=[pl.BlockSpec(memory_space=pltpu.SMEM), vm, vm, pl.BlockSpec(memory_space=pl.ANY)],
        out_specs=(pl.BlockSpec(memory_space=pl.ANY), vm, vm),
        scratch_shapes=[
            pltpu.VMEM((2, 4, 4, 4, 8, 1024), F32),
            pltpu.VMEM((1024, 1024), F32),
            pltpu.VMEM((NB, BS, BS), F32),
            pltpu.VMEM((1024, BS), F32),
            pltpu.VMEM((2, 4, 2, 32, 1024), F32),
            pltpu.VMEM((16, 2, 16, 1024), F32),
            pltpu.VMEM((2, 2, 16, 1024), F32),
            pltpu.VMEM((9, 16, 1024), F32),
            pltpu.VMEM((8, 16, 1024), F32),
            pltpu.VMEM((16, 16, 1024), F32),
            pltpu.VMEM((4, 512, 256), F32),
            pltpu.VMEM((4, 512, 256), F32),
            pltpu.VMEM((3, 512, 1024), BF16),
            pltpu.VMEM((3, 512, 1024), BF16),
            pltpu.VMEM((1024, 1024), BF16),
            pltpu.VMEM((1024, 1024), BF16),
            pltpu.VMEM((2, 512, 512), F32),
            sem((2,)), sem((2,)), sem((5,)),
            sem((2, 16)), sem((2, 4)), sem((8, 16)), sem((8, 16)), sem((8, 2)), sem((8, 2)),
            sem((8, 2)), sem((16,)), sem((2, 8, 2)), sem((2, 8, 2)), sem((1,)), sem((1,)),
            sem((2, 2, 4)), sem((2, 2, 4)), sem((16, 2)), sem((16, 2)),
            sem((4,)), sem((4,)),
        ],
        compiler_params=pltpu.CompilerParams(
            collective_id=0, has_side_effects=True, vmem_limit_bytes=60 << 20
        ),
    )(tile_map, diag_block.reshape(4, 8, 1024), panel_block, trailing[:, 0])
    return (updated[:, None], piece, diag)


def solution(mesh):
    in_specs = (P("row", "col", None, None), P("row", "col", None), P("row", None), P())
    out_specs = (P("row", "col", None, None), P("row", "col", None), P("row", None))
    return jax.shard_map(
        per_device, mesh=mesh, in_specs=in_specs, out_specs=out_specs, check_vma=False
    )
```

```python
import jax
import jax.numpy as jnp
from jax import lax
from jax.experimental import pallas as pl
from jax.experimental.pallas import tpu as pltpu
from jax.sharding import PartitionSpec as P

F32 = jnp.float32
BF16 = jnp.bfloat16
MESH = pl.DeviceIdType.MESH
NB = 8
BS = 128


def dot_nt(a, b):
    return lax.dot_general(
        a, b, (((1,), (1,)), ((), ())),
        precision=lax.Precision.HIGHEST, preferred_element_type=F32,
    )


def dot_nn(a, b):
    return lax.dot_general(
        a, b, (((1,), (0,)), ((), ())),
        precision=lax.Precision.HIGHEST, preferred_element_type=F32,
    )


def split(x):
    hi = x.astype(BF16)
    return hi, (x - hi.astype(F32)).astype(BF16)


def dot3(ah, al, bh, bl):
    def one(a, b):
        return lax.dot_general(
            a, b, (((1,), (1,)), ((), ())), preferred_element_type=F32
        )
    return one(ah, bh) + (one(ah, bl) + one(al, bh))


def factor_block(d_ref, w_ref, begin, end):
    iota = lax.broadcasted_iota(jnp.int32, (8, BS), 0)
    lane = lax.broadcasted_iota(jnp.int32, (8, BS), 1)
    groups = BS // 8

    def row(x, j):
        return jnp.broadcast_to(x[j:j + 1, :], (8, BS))

    def column(x, j):
        return jnp.broadcast_to(x[:, j:j + 1], (8, BS))

    if begin == 0:
        for q in range(groups):
            w_ref[8 * q:8 * q + 8, :] = jnp.where(lane == iota + 8 * q, 1.0, 0.0).astype(F32)
    for p in range(begin, end):
        base = 8 * p
        rows = slice(base, base + 8)
        d = d_ref[rows, :]
        w = w_ref[rows, :]
        cols = [column(d, base + k) for k in range(8)]
        inverse, pivots, heads = [], [], []
        for j in range(8):
            pivot = row(cols[j], j)
            inv = 1.0 / pivot
            pivots.append(pivot)
            inverse.append(inv)
            below = jnp.where(iota > j, cols[j], 0.0)
            head = [None] * 8
            for k in range(j + 1, 8):
                head[k] = row(cols[k], j)
                cols[k] = cols[k] - (below * head[k]) * inv
            heads.append(head)
            m = below * inv
            d = d - m * row(d, j)
            w = w - m * row(w, j)
        d_rows = [row(d, j) for j in range(8)]
        w_rows = [row(w, j) for j in range(8)]
        diag = pivots[7]
        for j in range(7):
            diag = jnp.where(iota == j, pivots[j], diag)
        scale = lax.rsqrt(diag)
        d_ref[rows, :] = jnp.where(lane >= iota + base, d * scale, 0.0)
        w_ref[rows, :] = w * scale
        for q in range(p + 1, groups):
            part = slice(8 * q, 8 * q + 8)
            dq = d_ref[part, :]
            wq = w_ref[part, :]
            cq = [column(dq, base + k) for k in range(8)]
            for j in range(8):
                mq = cq[j] * inverse[j]
                for k in range(j + 1, 8):
                    cq[k] = cq[k] - mq * heads[j][k]
                dq = dq - mq * d_rows[j]
                wq = wq - mq * w_rows[j]
            d_ref[part, :] = dq
            w_ref[part, :] = wq


def kernel(
    tm_ref, a_in, b_in, t_hbm,
    out_hbm, pf_out, df_out,
    a_ref, l_ref, w_ref, cbuf, rp, cp, bx, rsp, rsm, items,
    xs, xo, xhi, xlo, lhi, llo, tbuf,
    t_sem, o_sem, loc, s1, r1, s2, r2, s3, r3, sb, rb, srs, rrs, sx, rx, sag, rag, sa, ra,
    sxx, rxx,
):
    me_row = lax.axis_index("row")
    me_col = lax.axis_index("col")
    h, z = me_row // 16, me_row % 16
    l, y, k = me_col // 8, (me_col // 2) % 4, me_col % 2
    zq, zr = z // 4, z % 4
    turn = 2 * k + l
    plane = h * 8 + l * 4 + y
    chip = l * 4 + y
    sib = me_col + 1 - 2 * k

    def remote(src, dst, ssem, rsem, row, col):
        return pltpu.make_async_remote_copy(
            src_ref=src, dst_ref=dst, send_sem=ssem, recv_sem=rsem,
            device_id={"row": row, "col": col}, device_id_type=MESH,
        )

    def greet(row, col):
        pl.semaphore_signal(
            pltpu.get_barrier_semaphore(), inc=1,
            device_id={"row": row, "col": col}, device_id_type=MESH,
        )

    @pl.loop(0, 15)
    def _(i):
        d = 8 + (i + 1) // 2 * (1 - 2 * (i % 2))
        greet(h * 16 + (z + d) % 16, me_col)

    @pl.loop(1, 32)
    def _(d):
        q = (h * 16 + me_col + d) % 32
        greet((q // 16) * 16 + z, q % 16)

    def t_copy(g):
        slot = k if g == 0 else 1 - k
        return pltpu.make_async_copy(t_hbm.at[slot], tbuf.at[g], t_sem.at[g])

    def o_copy(g):
        slot = k if g == 0 else 1 - k
        return pltpu.make_async_copy(tbuf.at[g], out_hbm.at[slot], o_sem.at[g])

    for s in range(2):
        t_copy(s).start()

    pl.semaphore_wait(pltpu.get_barrier_semaphore(), 46)

    def lanes(J):
        return slice(BS * J, BS * J + BS)

    pieces = (slice(0, BS), slice(BS, NB * BS))

    def a1(n, d):
        return remote(a_in.at[y, :, pieces[n]], a_ref.at[h, zq, zr, y, :, pieces[n]],
                      s1.at[n, d], r1.at[n, zq], h * 16 + (z + d) % 16, me_col)

    def a_local(n):
        return pltpu.make_async_copy(
            a_in.at[y, :, pieces[n]], a_ref.at[h, zq, zr, y, :, pieces[n]], loc.at[n])

    def a1_start(n):
        @pl.when(zr == turn)
        def _():
            a_local(n).start()

            @pl.loop(0, 15)
            def _(i):
                a1(n, 8 + (i + 1) // 2 * (1 - 2 * (i % 2))).start()

    def a1_wait(n):
        @pl.loop(0, 4)
        def _(q):
            @pl.when(q * 4 + turn != z)
            def _():
                sl = a_ref.at[h, q, turn, y, :, pieces[n]]
                pltpu.make_async_copy(sl, sl, r1.at[n, q]).wait()

        @pl.when(zr == turn)
        def _():
            a_local(n).wait()

    def first(J, hh):
        return min(max(J - 4 * hh, 0), 4)

    def a2(J, hh, d):
        q = (plane + d) % 16
        sl = a_ref.at[hh, first(J, hh):4, turn, y, :, lanes(J)]
        return remote(sl, sl, s2.at[J, d], r2.at[J, plane],
                      (q // 8) * 16 + z, (q % 8) * 2 + k)

    def a2_each(J, act):
        for hh in range(2):
            if first(J, hh) < 4:
                @pl.when(h == hh)
                def _(hh=hh):
                    @pl.loop(1, 16)
                    def _(d):
                        act(a2(J, hh, d))

    def a2_start(J):
        a2_each(J, lambda c: c.start())

    def a2_sent(J):
        a2_each(J, lambda c: c.wait_send())

    def a2_wait(J):
        for hh in range(2):
            if first(J, hh) < 4:
                @pl.loop(0, 8)
                def _(c, hh=hh):
                    @pl.when(hh * 8 + c != plane)
                    def _():
                        sl = a_ref.at[hh, first(J, hh):4, 2 * k + c // 4, c % 4, :, lanes(J)]
                        pltpu.make_async_copy(sl, sl, r2.at[J, hh * 8 + c]).wait()

    def a3(J, hh, kk):
        sl = a_ref.at[hh, first(J, hh):4, pl.ds(2 * kk, 2), :, :, lanes(J)]
        return remote(sl, sl, s3.at[J, hh], r3.at[J, hh], me_row, sib)

    def halves(J):
        return [hh for hh in range(2) if first(J, hh) < 4]

    def a3_start(J):
        for hh in halves(J):
            a3(J, hh, k).start()

    def a3_wait(J):
        for hh in halves(J):
            a3(J, hh, 1 - k).wait_recv()

    def a3_sent(J):
        for hh in halves(J):
            a3(J, hh, k).wait_send()

    def b1(d, s):
        q = (chip + d) % 8
        return remote(b_in.at[s], rp.at[l, y, k], sb.at[d, s], rb.at[me_col],
                      me_row, q * 2 + s)

    def b_local():
        return pltpu.make_async_copy(b_in.at[k], rp.at[l, y, k], loc.at[2])

    def b1_each(act):
        for s in range(2):
            @pl.when(s != k)
            def _(s=s):
                act(b1(0, s))

            @pl.loop(1, 8)
            def _(d, s=s):
                act(b1(d, s))

    def b1_start():
        b_local().start()
        b1_each(lambda c: c.start())

    def b1_wait():
        b_local().wait()

        @pl.loop(0, 16)
        def _(c):
            @pl.when(c != me_col)
            def _():
                sl = rp.at[c // 8, (c // 2) % 4, c % 2]
                pltpu.make_async_copy(sl, sl, rb.at[c]).wait()

    v = (z + 16 - me_col) % 16
    right = h * 16 + (z + 1) % 16
    left = h * 16 + (z + 15) % 16
    NS = 2
    HR = 16
    ids = [tm_ref[2 * z], tm_ref[2 * z + 1], tm_ref[2 * z + 32], tm_ref[2 * z + 33]]

    def part(n):
        return pl.ds(n * (HR // NS), HR // NS)

    def swap():
        return remote(b_in.at[:, pl.ds((1 - h) * HR, HR)], bx.at[h], sx.at[0], rx.at[0],
                      (1 - h) * 16 + z, me_col)

    def swap_local():
        return pltpu.make_async_copy(b_in.at[:, pl.ds(h * HR, HR)], bx.at[h], loc.at[3])

    def swap_start():
        swap().start()
        swap_local().start()

    def swap_wait():
        swap_local().wait()
        sl = bx.at[1 - h]
        pltpu.make_async_copy(sl, sl, rx.at[0]).wait()

    def pick(item, n, value):
        for i in range(4):
            value = jnp.where(ids[i] == item, bx[i // 2, i % 2, part(n), :], value)
        return value

    def rs(way, t, n):
        buf = rsm if way else rsp
        return remote(buf.at[t, part(n)], buf.at[t + 1, part(n)],
                      srs.at[way, t, n], rrs.at[way, t, n], left if way else right, me_col)

    def rs_step(t):
        for n in range(NS):
            for way in range(2):
                if t < 8 - way:
                    buf = rsm if way else rsp
                    item = (v + 9 + t) % 16 if way else (v + 8 - t + 16) % 16
                    if t > 0:
                        rs(way, t - 1, n).wait_recv()
                        came = buf[t, part(n), :]
                    else:
                        came = bx[0, 0, part(n), :]
                    buf[t, part(n), :] = pick(item, n, came)
                    rs(way, t, n).start()

    def owner_of(item):
        def look(i, best):
            return jnp.where(tm_ref[i] == item, i, best)
        return lax.fori_loop(0, 64, look, jnp.int32(0))

    def ag_on(way, kind, t):
        return not (way == 1 and kind == 0 and t == 3)

    def ag(way, kind, t):
        item = (v + 2 * t) % 16 if way else (v - 2 * t + 16) % 16
        far = 2 - kind
        to = (z + 16 - far) % 16 if way else (z + far) % 16
        return remote(items.at[item], items.at[item], sag.at[way, kind, t],
                      rag.at[way, kind, t], h * 16 + to, me_col)

    def ag_start(t):
        for kind in range(2):
            for way in range(2):
                if ag_on(way, kind, t):
                    ag(way, kind, t).start()

    def ag_item(way, kind, t):
        far = 2 - kind + 2 * t
        return (v + far) % 16 if way else (v - far + 16) % 16

    def ag_wait(way, kind, t):
        sl = items.at[ag_item(way, kind, t)]
        pltpu.make_async_copy(sl, sl, rag.at[way, kind, t]).wait()

    def hand(item, hh):
        return remote(items.at[item], cp.at[me_col, h], sa.at[item, hh], ra.at[me_col, h],
                      hh * 16 + z, item)

    def hand_local():
        return pltpu.make_async_copy(items.at[me_col], cp.at[me_col, h], loc.at[4])

    def hand_each(item, act, act_local):
        if act_local is not None:
            @pl.when(item == me_col)
            def _():
                act_local(hand_local())

        @pl.when(item != me_col)
        def _():
            act(hand(item, h))
        act(hand(item, 1 - h))

    def hand_start(item):
        hand_each(item, lambda c: c.start(), lambda c: c.start())

    def collect():
        slot = owner_of(v)
        gap = ((slot // 2) % 16 - z + 16) % 16
        for n in range(NS):
            rs(0, 7, n).wait_recv()
            rs(1, 6, n).wait_recv()
            chain = jnp.where(gap >= 8, rsp[8, part(n), :], rsm[7, part(n), :])
            items[v, part(n), :] = pick(v, n, chain)
        ag_start(0)
        hand_start(v)

    def ag_step(t):
        arrived = [(way, kind) for kind in range(2) for way in range(2)
                   if ag_on(way, kind, t - 1)]
        for way, kind in arrived:
            if kind == 0:
                ag_wait(way, kind, t - 1)
        if t < 4:
            ag_start(t)
        for way, kind in arrived:
            if kind == 1:
                ag_wait(way, kind, t - 1)
        for way, kind in arrived:
            hand_start(ag_item(way, kind, t - 1))

    def hand_wait():
        hand_local().wait()
        for hh in range(2):
            @pl.loop(0, 16)
            def _(c, hh=hh):
                @pl.when((c != me_col) | (h != hh))
                def _():
                    pltpu.make_async_copy(cp.at[c, hh], cp.at[c, hh], ra.at[c, hh]).wait()

    def xx(m):
        return remote(xs.at[m], xo.at[m], sxx.at[m], rxx.at[m], me_row, sib)

    def sends_done():
        @pl.when(zr == turn)
        def _():
            for n in range(2):
                @pl.loop(1, 16)
                def _(d, n=n):
                    a1(n, d).wait_send()
        for J in range(NB):
            a2_sent(J)
            a3_sent(J)
        b1_each(lambda c: c.wait_send())
        swap().wait_send()
        for n in range(NS):
            for way in range(2):
                for t in range(8 - way):
                    rs(way, t, n).wait_send()
        for t in range(4):
            for kind in range(2):
                for way in range(2):
                    if ag_on(way, kind, t):
                        ag(way, kind, t).wait_send()

        @pl.loop(0, 16)
        def _(c):
            hand_each(c, lambda q: q.wait_send(), None)
        for m in range(4):
            xx(m).wait_send()

    def head():
        a1_start(0)
        swap_start()
        a1_start(1)
        swap_wait()
        rs_step(0)
        a1_wait(0)
        a2_start(0)
        rs_step(1)
        a1_wait(1)
        for J in range(1, 4):
            a2_start(J)
        rs_step(2)
        a2_wait(0)
        a3_start(0)
        for J in range(4, NB):
            a2_start(J)
        b1_start()
        rs_step(3)

    def tick(J, half):
        if half == 1 and J < NB - 1:
            a2_wait(J + 1)
            a3_start(J + 1)
        step = 2 * J + half + 3
        if 4 <= step <= 7:
            rs_step(step)
        elif step == 8:
            collect()
        elif half == 1 and 3 <= J <= 6:
            ag_step(J - 2)

    head()

    def block(I, J):
        return a_ref[I // 4, I % 4, :, :, :, lanes(J)].reshape(BS, BS)

    @pl.loop(0, NB)
    def _(Jd):
        for J in range(NB):
            @pl.when(Jd == J)
            def _(J=J):
                a3_wait(J)
                own = slice(BS * J, BS * J + BS)
                c = jnp.concatenate([block(I, J) for I in range(J, NB)], axis=0)
                if J > 0:
                    c = c - dot_nt(l_ref[BS * J:, :BS * J], l_ref[own, :BS * J])
                cbuf[:BS * (NB - J), :] = c
                tick(J, 0)
        factor_block(cbuf.at[0:BS], w_ref.at[Jd], 0, 8)
        for J in range(NB):
            @pl.when(Jd == J)
            def _(J=J):
                tick(J, 1)
        factor_block(cbuf.at[0:BS], w_ref.at[Jd], 8, 16)
        for J in range(NB):
            @pl.when(Jd == J)
            def _(J=J):
                own = slice(BS * J, BS * J + BS)
                l_ref[own, own] = cbuf[:BS, :].T
                if J < NB - 1:
                    low = slice(BS * (J + 1), NB * BS)
                    x = dot_nt(cbuf[BS:BS * (NB - J), :], w_ref[J])
                    l_ref[low, own] = x
                    lhi[low, own], llo[low, own] = split(x)

    start = pl.multiple_of(me_row * 32, 32)
    lane = lax.broadcasted_iota(jnp.int32, (32, NB * BS), 1)
    df_out[...] = jnp.where(lane < (me_row // 4 + 1) * BS, l_ref[pl.ds(start, 32), :], 0.0)
    b1_wait()
    wide_parts = []
    for m in range(4):
        cs = slice(256 * m, 256 * m + 256)
        w0, w1 = w_ref[2 * m], w_ref[2 * m + 1]
        l10 = l_ref[256 * m + BS:256 * m + 256, 256 * m:256 * m + BS]
        w10 = -dot_nn(w1, dot_nn(l10, w0))
        wide = jnp.concatenate([
            jnp.concatenate([w0, jnp.zeros_like(w0)], axis=1),
            jnp.concatenate([w10, w1], axis=1)], axis=0)
        wide_parts.append(split(wide))

    def solve(g, m):
        cs = slice(256 * m, 256 * m + 256)
        if g == 0:
            rows = rp[:, :, :, :, cs].reshape(512, 256)
        else:
            rows = cp[:, :, :, cs].reshape(512, 256)
        if m > 0:
            rows = rows - dot3(xhi[g, :, :256 * m], xlo[g, :, :256 * m],
                               lhi[cs, :256 * m], llo[cs, :256 * m])
        vh, vl = split(rows)
        x = dot3(vh, vl, *wide_parts[m])
        if g == 0:
            xs[m] = x
            xx(m).start()
        xhi[g, :, cs], xlo[g, :, cs] = split(x)

    for m in range(4):
        solve(0, m)
    hand_wait()
    for m in range(4):
        solve(1, m)

    def finish(g):
        t_copy(g).wait()
        slot = k if g == 0 else 1 - k
        live = tm_ref[2 * me_row + slot] >= me_col
        b = 2 * g
        prod = dot3(xhi[b], xlo[b], xhi[1], xlo[1])
        tbuf[g] = jnp.where(live, tbuf[g] - prod, 0.0)
        o_copy(g).start()

    finish(0)
    for m in range(4):
        cs = slice(256 * m, 256 * m + 256)
        xx(m).wait_recv()
        xhi[2, :, cs], xlo[2, :, cs] = split(xo[m])
    finish(1)
    mine = pl.ds(pl.multiple_of(me_col * 32, 32), 32)
    for m in range(4):
        cs = slice(256 * m, 256 * m + 256)
        own, other = xs[m, mine, :], xo[m, mine, :]
        pf_out[0, :, cs] = jnp.where(k == 0, own, other)
        pf_out[1, :, cs] = jnp.where(k == 0, other, own)
    sends_done()
    for g in range(2):
        o_copy(g).wait()


def per_device(trailing, panel_block, diag_block, tile_map):
    sem = pltpu.SemaphoreType.DMA
    vm = pl.BlockSpec(memory_space=pltpu.VMEM)
    updated, piece, diag = pl.pallas_call(
        kernel,
        out_shape=(
            jax.ShapeDtypeStruct((2, 512, 512), F32),
            jax.ShapeDtypeStruct((2, 32, 1024), F32),
            jax.ShapeDtypeStruct((32, 1024), F32),
        ),
        in_specs=[pl.BlockSpec(memory_space=pltpu.SMEM), vm, vm, pl.BlockSpec(memory_space=pl.ANY)],
        out_specs=(pl.BlockSpec(memory_space=pl.ANY), vm, vm),
        scratch_shapes=[
            pltpu.VMEM((2, 4, 4, 4, 8, 1024), F32),
            pltpu.VMEM((1024, 1024), F32),
            pltpu.VMEM((NB, BS, BS), F32),
            pltpu.VMEM((1024, BS), F32),
            pltpu.VMEM((2, 4, 2, 32, 1024), F32),
            pltpu.VMEM((16, 2, 16, 1024), F32),
            pltpu.VMEM((2, 2, 16, 1024), F32),
            pltpu.VMEM((9, 16, 1024), F32),
            pltpu.VMEM((8, 16, 1024), F32),
            pltpu.VMEM((16, 16, 1024), F32),
            pltpu.VMEM((4, 512, 256), F32),
            pltpu.VMEM((4, 512, 256), F32),
            pltpu.VMEM((3, 512, 1024), BF16),
            pltpu.VMEM((3, 512, 1024), BF16),
            pltpu.VMEM((1024, 1024), BF16),
            pltpu.VMEM((1024, 1024), BF16),
            pltpu.VMEM((2, 512, 512), F32),
            sem((2,)), sem((2,)), sem((5,)),
            sem((2, 16)), sem((2, 4)), sem((8, 16)), sem((8, 16)), sem((8, 2)), sem((8, 2)),
            sem((8, 2)), sem((16,)), sem((2, 8, 2)), sem((2, 8, 2)), sem((1,)), sem((1,)),
            sem((2, 2, 4)), sem((2, 2, 4)), sem((16, 2)), sem((16, 2)),
            sem((4,)), sem((4,)),
        ],
        compiler_params=pltpu.CompilerParams(
            collective_id=0, has_side_effects=True, vmem_limit_bytes=60 << 20
        ),
    )(tile_map, diag_block.reshape(4, 8, 1024), panel_block, trailing[:, 0])
    return (updated[:, None], piece, diag)


def solution(mesh):
    in_specs = (P("row", "col", None, None), P("row", "col", None), P("row", None), P())
    out_specs = (P("row", "col", None, None), P("row", "col", None), P("row", None))
    return jax.shard_map(
        per_device, mesh=mesh, in_specs=in_specs, out_specs=out_specs, check_vma=False
    )
```
